128 devices in a mesh: blk: 16 (over y, x), sims: 8 (over z, core).
Axes of the slice: x: 4, y: 4, z: 4, core: 2. Of those that a mesh axis runs over, the one named last changes fastest.
Arguments:
- rhs: float32 [4, 16, 256, 1024], P(None, 'blk', None, 'sims'), parts along dimension 3, may hold values from -6 to 6
- lower_blocks: float32 [4, 16, 3, 256, 256], P(None, 'blk'), may hold values from -0.16875 to 0.16875
- col_index: int32 [4, 16, 3], P(None, 'blk'), may hold values from -1 to 62, as said below
- diag_inverse: float32 [4, 16, 256, 256], P(None, 'blk'), may hold values from -1.5 to 1.5, as said below
- turnout: float32 [4, 16, 256], P(None, 'blk'), may hold values from 0.2 to 5
- district_of: int32 [4, 16, 256], P(None, 'blk'), may hold values from 0 to 255, as said below
Outputs:
- solution: float32 [4, 16, 256, 1024], P(None, 'blk', None, 'sims'), parts along dimension 3
- district_mean: float32 [256, 1024], P('blk', 'sims'), parts along dimension 1
The draws below stay inside these ranges and needn't reach their ends.
There are 8 independent parts, one for each index of `sims`. The reference program is written for one: setup_inputs(seed, part) draws one part's arguments, and reference() takes and returns one part's arrays. A program takes and returns all parts, laid end to end along the dimension named above; an argument that names none is the same for every part. Nothing has to cross between parts.
Inputs may be any that keep to these rules, and one draw needn't show every extreme that they name: `col_index`: entry [r, p, k] belongs to block row i = r * 16 + p. Slot 0 holds i - 1 (-1 for i = 0); the other slots hold distinct columns from i - 4 to i - 2, or -1 where the block is absent. `diag_inverse`: each block is lower triangular. `district_of`: each district holds exactly 64 precincts.
All inputs are finite; a program needn't handle non-finite values.
Results may differ from the reference program's by a relative error of at most 0.0002.
Values sent between devices are 32-bit elements; how exact they have to be, the bound alone decides.
A program may use at most 64 MiB of HBM per device.

```python
import math
import jax
import jax.numpy as jnp
from jax import lax

BS = 256
SIMS = 128
ROWS_DEV = 4
KMAX = 3
WIN = 4
NDIST = 256
N_BLK = 16


def draw_lower_blocks(key, part):
    shape_full = (ROWS_DEV, N_BLK, KMAX, BS, BS)
    values = jnp.clip(jax.random.normal(key, shape_full, jnp.float32), -4.0, 4.0) * (0.675 * BS ** (-0.5))
    return values.astype(jnp.float32)


def draw_col_index(key, part):
    first_key, second_key = jax.random.split(key)
    row_number = jnp.arange(ROWS_DEV, dtype=jnp.int32)[:, None] * N_BLK + jnp.arange(N_BLK, dtype=jnp.int32)[None, :]
    scores = jax.random.randint(first_key, (ROWS_DEV, N_BLK, WIN - 1), 0, 4096) * WIN + jnp.arange(WIN - 1, dtype=jnp.int32)
    ranking = jnp.argsort(scores, axis=-1).astype(jnp.int32)
    offsets = ranking[..., :KMAX - 1] + 2
    keep_flag = jax.random.randint(second_key, (ROWS_DEV, N_BLK, KMAX - 1), 0, 2)
    extra_columns = row_number[..., None] - offsets
    extra_columns = jnp.where((keep_flag == 1) & (extra_columns >= 0), extra_columns, -1)
    first_column = jnp.where(row_number >= 1, row_number - 1, -1)
    return jnp.concatenate([first_column[..., None], extra_columns], axis=-1).astype(jnp.int32)


def draw_diag_inverse(key, part):
    diag_key, lower_key = jax.random.split(key)
    diagonal = jax.random.uniform(diag_key, (ROWS_DEV, N_BLK, BS), jnp.float32, 0.6, 1.2)
    lower_part = jnp.clip(jax.random.normal(lower_key, (ROWS_DEV, N_BLK, BS, BS), jnp.float32), -4.0, 4.0) * (0.6 * BS ** (-0.5))
    strict_lower = jnp.tril(jnp.ones((BS, BS), jnp.float32), -1)
    identity = jnp.eye(BS, dtype=jnp.float32)
    return lower_part * strict_lower + identity * diagonal[..., :, None]


def draw_district_of(key, part):
    shuffled = jax.random.permutation(key, ROWS_DEV * N_BLK * BS).astype(jnp.int32)
    return (shuffled % NDIST).reshape(ROWS_DEV, N_BLK, BS).astype(jnp.int32)


def levels(key, extent, shards, low, high):
    def one(position, parts):
        steps = jax.random.uniform(jax.random.fold_in(jax.random.fold_in(key, 6), position), (parts,), jnp.float32, low / len(shards), high / len(shards))
        return jnp.repeat(jnp.exp(steps), extent[position] // parts).reshape((-1,) + (1,) * (len(extent) - position - 1))

    factor_of = one(*shards[0])
    for cut in shards[1:]:
        factor_of = factor_of * one(*cut)
    return factor_of


def scatter_about(own_key, shape, deviation, most, cuts=(), held_as=jnp.bfloat16):
    gain = levels(own_key, shape, cuts, -0.22, 0.18) if cuts else 1.0
    array = jax.random.normal(own_key, shape, jnp.float32) * deviation * gain
    return jnp.minimum(jnp.maximum(array, -most), most).astype(held_as)


def setup_inputs(seed: int = 0, part: int = 0) -> dict:
    splits = jax.random.split(jax.random.key(seed), 7)
    own_keys = jax.random.split(jax.random.fold_in(splits[6], part), 7)
    rhs = scatter_about(own_keys[0], (ROWS_DEV, N_BLK, BS, SIMS), 1.0, 6.0, ((1, 16),), jnp.float32)
    lower_blocks = draw_lower_blocks(jax.random.fold_in(splits[6], 71), part)
    col_index = draw_col_index(jax.random.fold_in(splits[6], 71), part)
    diag_inverse = draw_diag_inverse(jax.random.fold_in(splits[6], 71), part)
    turnout = jnp.clip(jnp.exp(math.log(5.0) - 3.218876 * jax.random.uniform(splits[4], (ROWS_DEV, N_BLK, BS), jnp.float32) ** levels(splits[4], (ROWS_DEV, N_BLK, BS), ((1, 16),), -0.2, 0.2)), 0.2, 5.0)
    district_of = draw_district_of(jax.random.fold_in(splits[6], 71), part)
    return {"rhs": rhs, "lower_blocks": lower_blocks, "col_index": col_index, "diag_inverse": diag_inverse, "turnout": turnout, "district_of": district_of}


precise = lax.Precision.HIGHEST


def reference(rhs, lower_blocks, col_index, diag_inverse, turnout, district_of):
    total_rows = ROWS_DEV * N_BLK
    rhs_rows = rhs.reshape(total_rows, BS, SIMS)
    factor_rows = lower_blocks.reshape(total_rows, KMAX, BS, BS)
    column_rows = col_index.reshape(total_rows, KMAX)
    inverse_rows = diag_inverse.reshape(total_rows, BS, BS)

    def advance(count, loop_state):
        solution, pending = loop_state
        row_now = (total_rows - 1 - count).astype(jnp.int32)
        solved = jnp.einsum('ab,as->bs', inverse_rows[row_now], rhs_rows[row_now] - pending[row_now], precision=precise)
        solution = solution.at[row_now].set(solved)
        for slot_index in range(KMAX):
            target = column_rows[row_now, slot_index]
            update_term = jnp.einsum('ab,as->bs', factor_rows[row_now, slot_index], solved, precision=precise)
            update_term = jnp.where(target >= 0, update_term, jnp.zeros_like(update_term))
            pending = pending.at[jnp.maximum(target, 0)].add(update_term)
        return solution, pending

    empty_rows = jnp.zeros((total_rows, BS, SIMS), jnp.float32)
    solution, _ = lax.fori_loop(0, total_rows, advance, (empty_rows, empty_rows))
    cell_rows = solution.reshape(total_rows * BS, SIMS)
    weights = turnout.reshape(total_rows * BS)
    district_ids = district_of.reshape(total_rows * BS)
    numerator = jax.ops.segment_sum(weights[:, None] * cell_rows, district_ids, num_segments=NDIST)
    denominator = jax.ops.segment_sum(weights, district_ids, num_segments=NDIST)
    return solution.reshape(ROWS_DEV, N_BLK, BS, SIMS), numerator / denominator[:, None]
```

```python
import jax
import jax.numpy as jnp
from jax import lax
from jax.experimental import pallas as pl
from jax.experimental.pallas import tpu as pltpu
from jax.sharding import PartitionSpec as P

MESH = pl.DeviceIdType.MESH
F32 = jnp.float32
BF16 = jnp.bfloat16

BS = 256
ROWS = 4
KMAX = 3
COLS = 128
NB = 16
NDIST = 256
SHARE = NDIST // NB
GROUP = 8
PIECES = 4
WIDTH = COLS // PIECES
HALF = COLS // 2


def split(value):
    high = value.astype(BF16)
    return high, (value - high.astype(F32)).astype(BF16)


def dot(a, b):
    return jnp.dot(a, b, preferred_element_type=F32)


def landed(ref, sem):
    pltpu.make_async_copy(ref, ref, sem).wait()


def kernel(
    rhs_ref, lower_ref, col_ref, diag_ref, turn_ref, dist_ref,
    sol_ref, mean_ref,
    diag_high, diag_low, push_out, side_out, push_in, side_in, push_high, push_low,
    zeta, zeta_in, edge_in, edge_out, numer, numer_in, denom, denom_in,
    push_sent, push_got, side_sent, side_got, edge_sent, edge_got,
    zeta_sent, zeta_got, numer_sent, numer_got, denom_sent, denom_got,
):
    b = lax.axis_index("blk")
    s = lax.axis_index("sims")
    y, x = lax.div(b, 4), lax.rem(b, 4)
    core = lax.rem(s, 2)
    plane = s - core

    barrier = pltpu.get_barrier_semaphore()

    def greet(step, carry):
        other = lax.rem(b * 2 + core + step, 32)
        pl.semaphore_signal(
            barrier, inc=1,
            device_id={"blk": lax.div(other, 2), "sims": plane + lax.rem(other, 2)},
            device_id_type=MESH,
        )
        return carry

    lax.fori_loop(1, 32, greet, 0)

    upper = lax.div(y, 2)
    own_y = jnp.where(upper == 1, 2 + core, 1 - core)
    slot = 4 * lax.rem(y, 2) + x

    def prepare(r):
        high, low = split(diag_ref[r])
        diag_high[r] = high
        diag_low[r] = low
        both = jnp.concatenate([high, low], 0)
        for k in range(KMAX):
            l_high, l_low = split(lower_ref[r, k])
            wide = dot(both, l_high)
            push_out[r, k] = wide[:BS] + (wide[BS:] + dot(high, l_low))
        side_out[r, :COLS] = rhs_ref[r].T
        row = 16 * r + b
        masks = []
        for k in (1, 2):
            column = jnp.full((1, BS), col_ref[r, k], jnp.int32)
            for d in (2, 3, 4):
                masks.append(jnp.where((column >= 0) & (column == row - d), 1.0, 0.0).astype(F32))
        masks.append(jnp.zeros((2, BS), F32))
        side_out[r, COLS:] = jnp.concatenate(masks, 0)

    def pieces_of(r):
        to = {"blk": 4 * own_y + r, "sims": plane + 1}
        return (
            (side_out.at[r], side_in.at[slot], side_sent.at[r], side_got.at[slot], to),
            (push_out.at[r], push_in.at[slot], push_sent.at[r], push_got.at[slot], to),
        )

    def stays(r):
        return (core == 1) & (4 * own_y + r == b)

    def hand_over(r):
        @pl.when(stays(r))
        def _():
            for src, dst, _, got, _ in pieces_of(r):
                pltpu.make_async_copy(src, dst, got).start()

        @pl.when(jnp.logical_not(stays(r)))
        def _():
            for src, dst, sent, got, to in pieces_of(r):
                pltpu.make_async_remote_copy(src, dst, sent, got, device_id=to, device_id_type=MESH).start()

    prepare(3)
    pl.semaphore_wait(barrier, 31)
    hand_over(3)

    def prepare_next(step, carry):
        r = 2 - step
        prepare(r)
        hand_over(r)
        return carry

    lax.fori_loop(0, 3, prepare_next, 0)

    def members(r):
        ids = dist_ref[pl.ds(r, 1), :]
        return lax.broadcasted_iota(jnp.int32, (NDIST, BS), 0) == ids

    weight = jnp.zeros((NDIST, BS), F32)
    for r in range(ROWS):
        weight = weight + jnp.where(members(r), turn_ref[r : r + 1, :], 0.0)
    denom[...] = jnp.broadcast_to(jnp.sum(weight, 1, keepdims=True), (NDIST, COLS))
    numer[...] = jnp.zeros_like(numer)

    def exchange(source, target, sent, got):
        def one(step, carry):
            other = lax.rem(b + step, NB)
            pltpu.make_async_remote_copy(
                source.at[pl.ds(SHARE * other, SHARE)], target.at[b], sent.at[other], got.at[b],
                device_id={"blk": other, "sims": s}, device_id_type=MESH,
            ).start()
            return carry

        lax.fori_loop(1, NB, one, 0)
        target[b] = source[pl.ds(pl.multiple_of(SHARE * b, SHARE), SHARE), :]

    def exchanged(source, target, sent, got):
        def one(step, carry):
            other = lax.rem(b + step, NB)
            landed(target.at[other], got.at[other])
            landed(source.at[pl.ds(SHARE * other, SHARE)], sent.at[other])
            return carry

        lax.fori_loop(1, NB, one, 0)

    exchange(denom, denom_in, denom_sent, denom_got)

    def finish(r):
        for part in range(2):
            landed(zeta_in.at[r, pl.ds(HALF * part, HALF)], zeta_got.at[r, part])
        high, low = split(zeta_in[r])
        both = jnp.concatenate([high, low], 0)
        wide = dot(both, diag_high[r])
        field = wide[:COLS] + (wide[COLS:] + dot(high, diag_low[r]))
        sol_ref[r] = field.T
        w_high, w_low = split(field * turn_ref[pl.ds(r, 1), :])
        member = jnp.where(members(r), 1.0, 0.0).astype(BF16)
        contract = (((1,), (1,)), ((), ()))
        numer[...] += lax.dot_general(
            member, w_high, contract, preferred_element_type=F32
        ) + lax.dot_general(member, w_low, contract, preferred_element_type=F32)

    def finish_down(step, carry):
        finish(3 - step)
        return carry

    @pl.when(core == 0)
    def _():
        lax.fori_loop(0, ROWS, finish_down, 0)

    @pl.when(core == 1)
    def _():
        half = lax.div(y, 2)
        part = jnp.where(half == 1, lax.rem(y, 2), 1 - lax.rem(y, 2))
        is_first = (half == 1) & (x == 3)
        is_last = (half == 0) & (x == 0)
        next_b = jnp.where(half == 1, 4 * (1 - part) + x, 4 * (2 + part) + x - 1)

        early = jnp.maximum(2 - x, 0)
        lax.fori_loop(0, early, finish_down, 0)

        def receive(step, carry):
            t = GROUP - 1 - step
            landed(side_in.at[t], side_got.at[t])
            landed(push_in.at[t], push_got.at[t])
            for k in range(KMAX):
                high, low = split(push_in[t, k])
                push_high[t, k] = high
                push_low[t, k] = low
            return carry

        lax.fori_loop(0, GROUP, receive, 0)

        def edge_copies(p):
            to = {"blk": next_b, "sims": s}
            return [
                pltpu.make_async_remote_copy(
                    edge_out.at[p, lo:hi], edge_in.at[p, lo:hi], edge_sent.at[p, n], edge_got.at[p, n],
                    device_id=to, device_id_type=MESH,
                )
                for n, (lo, hi) in enumerate(((0, 1), (1, 4)))
            ]

        def home(t):
            return 4 * (2 * half + lax.div(t, 4)) + lax.rem(t, 4)

        def is_home(t):
            return (part == 1) & (home(t) == b)

        def return_zeta(t, n):
            src = zeta.at[t, pl.ds(HALF * n, HALF)]
            dst = zeta_in.at[x, pl.ds(HALF * n, HALF)]

            @pl.when(is_home(t))
            def _():
                pltpu.make_async_copy(src, dst, zeta_got.at[x, n]).start()

            @pl.when(jnp.logical_not(is_home(t)))
            def _():
                pltpu.make_async_remote_copy(
                    src, dst, zeta_sent.at[t, n], zeta_got.at[x, n],
                    device_id={"blk": home(t), "sims": plane + part}, device_id_type=MESH,
                ).start()

        def piece(p, carry):
            here = pl.ds(pl.multiple_of(WIDTH * p, WIDTH), WIDTH)

            @pl.when(is_first)
            def _():
                edge_in[p] = jnp.zeros((4, WIDTH, BS), F32)

            @pl.when(jnp.logical_not(is_first))
            def _():
                landed(edge_in.at[p, 0:1], edge_got.at[p, 0])
                landed(edge_in.at[p, 1:4], edge_got.at[p, 1])

            pending = [edge_in[p, d] for d in range(4)]
            for t in reversed(range(GROUP)):
                z = side_in[t, here, :] - pending[0]
                zeta[t, here, :] = z
                high, low = split(z)
                both = jnp.concatenate([high, low], 0)
                updates = []
                for k in range(KMAX):
                    wide = dot(both, push_high[t, k])
                    updates.append(wide[:WIDTH] + (wide[WIDTH:] + dot(high, push_low[t, k])))
                moved = [pending[1] + updates[0]]
                for d in range(3):
                    base = pending[2 + d] if d < 2 else jnp.zeros((WIDTH, BS), F32)
                    first = side_in[t, COLS + d : COLS + d + 1, :] > 0.5
                    second = side_in[t, COLS + 3 + d : COLS + 4 + d, :] > 0.5
                    moved.append(
                        base + jnp.where(first, updates[1], jnp.where(second, updates[2], 0.0))
                    )
                pending = moved
            for d in range(4):
                edge_out[p, d] = pending[d]

            @pl.when(jnp.logical_not(is_last))
            def _():
                for copy in edge_copies(p):
                    copy.start()

            @pl.when(lax.rem(p, 2) == 1)
            def _():
                def one(step, c):
                    return_zeta(GROUP - 1 - step, lax.div(p, 2))
                    return c

                lax.fori_loop(0, GROUP, one, 0)

            return carry

        lax.fori_loop(0, PIECES, piece, 0)
        lax.fori_loop(early, ROWS, finish_down, 0)

        @pl.when(jnp.logical_not(is_last))
        def _():
            for p in range(PIECES):
                for copy in edge_copies(p):
                    copy.wait_send()

        def sent_one(step, c):
            t, n = lax.div(step, 2), lax.rem(step, 2)

            @pl.when(jnp.logical_not(is_home(t)))
            def _():
                landed(zeta.at[t, pl.ds(HALF * n, HALF)], zeta_sent.at[t, n])

            return c

        lax.fori_loop(0, 2 * GROUP, sent_one, 0)

    exchange(numer, numer_in, numer_sent, numer_got)

    def handed(r, carry):
        @pl.when(jnp.logical_not(stays(r)))
        def _():
            for src, _, sent, _, _ in pieces_of(r):
                landed(src, sent)

        return carry

    lax.fori_loop(0, ROWS, handed, 0)
    exchanged(denom, denom_in, denom_sent, denom_got)
    exchanged(numer, numer_in, numer_sent, numer_got)
    mean_ref[...] = jnp.sum(numer_in[...], 0) / jnp.sum(denom_in[...], 0)


def body(rhs, lower_blocks, col_index, diag_inverse, turnout, district_of):
    vmem = pl.BlockSpec(memory_space=pltpu.VMEM)
    dma = pltpu.SemaphoreType.DMA
    field, mean = pl.pallas_call(
        kernel,
        out_shape=(
            jax.ShapeDtypeStruct((ROWS, BS, COLS), F32),
            jax.ShapeDtypeStruct((SHARE, COLS), F32),
        ),
        in_specs=[vmem, vmem, pl.BlockSpec(memory_space=pltpu.SMEM), vmem, vmem, vmem],
        out_specs=(vmem, vmem),
        scratch_shapes=[
            pltpu.VMEM((ROWS, BS, BS), BF16),
            pltpu.VMEM((ROWS, BS, BS), BF16),
            pltpu.VMEM((ROWS, KMAX, BS, BS), F32),
            pltpu.VMEM((ROWS, COLS + 8, BS), F32),
            pltpu.VMEM((GROUP, KMAX, BS, BS), F32),
            pltpu.VMEM((GROUP, COLS + 8, BS), F32),
            pltpu.VMEM((GROUP, KMAX, BS, BS), BF16),
            pltpu.VMEM((GROUP, KMAX, BS, BS), BF16),
            pltpu.VMEM((GROUP, COLS, BS), F32),
            pltpu.VMEM((ROWS, COLS, BS), F32),
            pltpu.VMEM((PIECES, 4, WIDTH, BS), F32),
            pltpu.VMEM((PIECES, 4, WIDTH, BS), F32),
            pltpu.VMEM((NDIST, COLS), F32),
            pltpu.VMEM((NB, SHARE, COLS), F32),
            pltpu.VMEM((NDIST, COLS), F32),
            pltpu.VMEM((NB, SHARE, COLS), F32),
            dma((ROWS,)), dma((GROUP,)), dma((ROWS,)), dma((GROUP,)),
            dma((PIECES, 2)), dma((PIECES, 2)),
            dma((GROUP, 2)), dma((ROWS, 2)),
            dma((NB,)), dma((NB,)), dma((NB,)), dma((NB,)),
        ],
        name="back_substitution",
        compiler_params=pltpu.CompilerParams(
            collective_id=0, has_side_effects=True, vmem_limit_bytes=48 * 1024 * 1024
        ),
    )(
        rhs[:, 0], lower_blocks[:, 0], col_index[:, 0], diag_inverse[:, 0], turnout[:, 0], district_of[:, 0]
    )
    return field[:, None], mean


def solution(mesh):
    placed = (
        P(None, "blk", None, "sims"),
        P(None, "blk", None, None, None),
        P(None, "blk", None),
        P(None, "blk", None, None),
        P(None, "blk", None),
        P(None, "blk", None),
    )
    return jax.shard_map(
        body,
        mesh=mesh,
        in_specs=placed,
        out_specs=(P(None, "blk", None, "sims"), P("blk", "sims")),
        check_vma=False,
    )
```

```python
import jax
import jax.numpy as jnp
from jax import lax
from jax.experimental import pallas as pl
from jax.experimental.pallas import tpu as pltpu
from jax.sharding import PartitionSpec as P

MESH = pl.DeviceIdType.MESH
F32 = jnp.float32
BF16 = jnp.bfloat16

BS = 256
ROWS = 4
KMAX = 3
COLS = 128
NB = 16
NDIST = 256
SHARE = NDIST // NB
GROUP = 8
PIECES = 4
WIDTH = COLS // PIECES
HALF = COLS // 2


def split(value):
    high = value.astype(BF16)
    return high, (value - high.astype(F32)).astype(BF16)


def dot(a, b):
    return jnp.dot(a, b, preferred_element_type=F32)


def landed(ref, sem):
    pltpu.make_async_copy(ref, ref, sem).wait()


def in_hbm(array):
    return pltpu.with_memory_space_constraint(array, pltpu.HBM)


def kernel(
    rhs_hbm, lower_hbm, col_ref, diag_hbm, turn_ref, dist_ref,
    sol_ref, mean_ref,
    rhs_ref, lower_ref, diag_ref,
    diag_high, diag_low, push_out, side_out, push_in, side_in, push_high, push_low,
    zeta, zeta_in, edge_in, edge_out, numer, numer_in, denom, denom_in,
    read_got, push_sent, push_got, pass_sent, pass_got, side_sent, side_got, edge_sent, edge_got,
    zeta_sent, zeta_got, numer_sent, numer_got, denom_sent, denom_got,
):
    b = lax.axis_index("blk")
    s = lax.axis_index("sims")
    y, x = lax.div(b, 4), lax.rem(b, 4)
    core = lax.rem(s, 2)
    plane = s - core
    z_here = lax.div(s, 2)
    mine = pl.multiple_of(128 * lax.rem(z_here, 2), 128)

    def reads(r):
        return (
            pltpu.make_async_copy(diag_hbm.at[r, 0], diag_ref.at[r], read_got.at[r, 0]),
            pltpu.make_async_copy(lower_hbm.at[r, 0], lower_ref.at[r], read_got.at[r, 1]),
            pltpu.make_async_copy(rhs_hbm.at[r, 0], rhs_ref.at[r], read_got.at[r, 2]),
        )

    def start_reads(step, carry):
        for copy in reads(3 - step):
            copy.start()
        return carry

    lax.fori_loop(0, ROWS, start_reads, 0)

    barrier = pltpu.get_barrier_semaphore()

    def hail(other_blk, other_sims):
        pl.semaphore_signal(barrier, inc=1, device_id={"blk": other_blk, "sims": other_sims}, device_id_type=MESH)

    upper = lax.div(y, 2)
    lane = jnp.where(upper == 1, lax.rem(y, 2), 1 - lax.rem(y, 2))

    def greet(step, carry):
        hail(lax.rem(b + step, NB), s)
        return carry

    lax.fori_loop(1, NB, greet, 0)

    @pl.when(core == 0)
    def _():
        for r in range(ROWS):
            hail(4 * jnp.where(upper == 1, 2, 1) + r, plane + 1)

    @pl.when((core == 1) & (lane == 0))
    def _():
        for t in range(GROUP):
            hail(8 * upper + t, plane)

    above = plane + core + 2 - 8 * lax.div(plane + 2, 8)
    below = lax.rem(plane + 6, 8) + core
    for other in (above, below):
        pl.semaphore_signal(barrier, inc=1, device_id={"blk": b, "sims": other}, device_id_type=MESH)

    upper = lax.div(y, 2)
    own_y = jnp.where(upper == 1, 2 + core, 1 - core)
    slot = 4 * lax.rem(y, 2) + x

    def prepare_side(r):
        for copy in reads(r):
            copy.wait()
        high, low = split(diag_ref[r])
        diag_high[r] = high
        diag_low[r] = low
        side_out[r, :COLS] = rhs_ref[r].T
        row = 16 * r + b
        masks = []
        for k in (1, 2):
            column = jnp.full((1, BS), col_ref[k, 0, r], jnp.int32)
            for d in (2, 3, 4):
                masks.append(jnp.where((column >= 0) & (column == row - d), 1.0, 0.0).astype(F32))
        masks.append(jnp.zeros((2, BS), F32))
        side_out[r, COLS:] = jnp.concatenate(masks, 0)

    def prepare(r, k):
        high, low = diag_high[r, pl.ds(mine, 128), :], diag_low[r, pl.ds(mine, 128), :]
        both = jnp.concatenate([high, low], 0)
        l_high, l_low = split(lower_ref[r, k])
        wide = dot(both, l_high)
        push_out[r, k] = wide[:128] + (wide[128:] + dot(high, l_low))

    def side_of(r):
        return side_out.at[r], side_in.at[slot], side_sent.at[r], side_got.at[slot]

    def push_of(r, k):
        return push_out.at[r, k], push_in.at[slot, k, pl.ds(mine, 128)], push_sent.at[r, k], push_got.at[slot, k]

    def stays(r):
        return (core == 1) & (4 * own_y + r == b)

    def hand_over(r, what):
        src, dst, sent, got = what

        @pl.when(stays(r))
        def _():
            pltpu.make_async_copy(src, dst, got).start()

        @pl.when(jnp.logical_not(stays(r)))
        def _():
            to = {"blk": 4 * own_y + r, "sims": plane + 1}
            pltpu.make_async_remote_copy(src, dst, sent, got, device_id=to, device_id_type=MESH).start()

    def quarter(t, k, n):
        where = push_in.at[t, k, pl.ds(mine + 64 * n, 64)]
        return pltpu.make_async_remote_copy(
            where, where, pass_sent.at[t, k, n], pass_got.at[t, k, n],
            device_id={"blk": b, "sims": (above, below)[n]}, device_id_type=MESH,
        )

    def keep(t, k, start):
        rows = pl.ds(start, 128)
        high, low = split(push_in[t, k, rows, :])
        push_high[t, k, rows, :] = high
        push_low[t, k, rows, :] = low

    def forward(step, carry):
        k, t = lax.div(step, GROUP), GROUP - 1 - lax.rem(step, GROUP)
        landed(push_in.at[t, k, pl.ds(mine, 128)], push_got.at[t, k])
        for n in range(2):
            quarter(t, k, n).start()
        keep(t, k, mine)
        return carry

    def forward_all(k):
        def one(step, carry):
            forward(k * GROUP + step, 0)
            return carry

        lax.fori_loop(0, GROUP, one, 0)

    def sent(r, refs):
        @pl.when(jnp.logical_not(stays(r)))
        def _():
            for ref, sem in refs:
                landed(ref, sem)

    def sent_push(k):
        def one(r, carry):
            sent(r, [(push_out.at[r, k], push_sent.at[r, k])])
            return carry

        lax.fori_loop(0, ROWS, one, 0)

    def prepare_all(k):
        def one(step, carry):
            r = 3 - step
            prepare(r, k)
            hand_over(r, push_of(r, k))
            return carry

        lax.fori_loop(0, ROWS, one, 0)

    prepare_side(3)
    prepare(3, 0)
    pl.semaphore_wait(barrier, NB + 1 + jnp.where(core == 0, ROWS, jnp.where(lane == 0, GROUP, 0)))
    hand_over(3, push_of(3, 0))

    def prepare_first(step, carry):
        r = 2 - step
        prepare_side(r)
        prepare(r, 0)
        hand_over(r, push_of(r, 0))
        return carry

    lax.fori_loop(0, 3, prepare_first, 0)
    prepare_all(1)

    @pl.when(core == 1)
    def _():
        forward_all(0)


    prepare_all(2)
    hand_over(3, side_of(3))

    @pl.when(core == 1)
    def _():
        forward_all(1)

    sent_push(0)
    sent_push(1)
    sent_push(2)
    for r in (2, 1, 0):
        hand_over(r, side_of(r))

    @pl.when(core == 1)
    def _():
        forward_all(2)

    def members(r):
        ids = dist_ref[r]
        return lax.broadcasted_iota(jnp.int32, (NDIST, BS), 0) == ids

    numer[...] = jnp.zeros_like(numer)

    def exchange(source, target, sent, got):
        def one(step, carry):
            other = lax.rem(b + step, NB)
            pltpu.make_async_remote_copy(
                source.at[pl.ds(SHARE * other, SHARE)], target.at[b], sent.at[other], got.at[b],
                device_id={"blk": other, "sims": s}, device_id_type=MESH,
            ).start()
            return carry

        lax.fori_loop(1, NB, one, 0)
        target[b] = source[pl.ds(pl.multiple_of(SHARE * b, SHARE), SHARE), :]

    def exchanged(source, target, sent, got):
        def one(step, carry):
            other = lax.rem(b + step, NB)
            landed(target.at[other], got.at[other])
            landed(source.at[pl.ds(SHARE * other, SHARE)], sent.at[other])
            return carry

        lax.fori_loop(1, NB, one, 0)

    def share_weights():
        weight = jnp.zeros((NDIST, BS), F32)
        for r in range(ROWS):
            weight = weight + jnp.where(members(r), turn_ref[r], 0.0)
        denom[...] = jnp.broadcast_to(jnp.sum(weight, 1, keepdims=True), (NDIST, COLS))
        exchange(denom, denom_in, denom_sent, denom_got)

    @pl.when((core == 0) | (x < 3))
    def _():
        share_weights()

    def finish(r):
        for part in range(2):
            landed(zeta_in.at[r, pl.ds(HALF * part, HALF)], zeta_got.at[r, part])
        high, low = split(zeta_in[r])
        both = jnp.concatenate([high, low], 0)
        wide = dot(both, diag_high[r])
        field = wide[:COLS] + (wide[COLS:] + dot(high, diag_low[r]))
        sol_ref[r] = field.T
        w_high, w_low = split(field * turn_ref[r])
        member = jnp.where(members(r), 1.0, 0.0).astype(BF16)
        contract = (((1,), (1,)), ((), ()))
        numer[...] += lax.dot_general(
            member, w_high, contract, preferred_element_type=F32
        ) + lax.dot_general(member, w_low, contract, preferred_element_type=F32)

    def finish_down(step, carry):
        finish(3 - step)
        return carry

    @pl.when(core == 0)
    def _():
        lax.fori_loop(0, ROWS, finish_down, 0)

    @pl.when(core == 1)
    def _():
        half = lax.div(y, 2)
        part = jnp.where(half == 1, lax.rem(y, 2), 1 - lax.rem(y, 2))
        is_first = (half == 1) & (x == 3)
        is_last = (half == 0) & (x == 0)
        next_b = jnp.where(half == 1, 4 * (1 - part) + x, 4 * (2 + part) + x - 1)

        early = jnp.maximum(2 - x, 0)
        theirs = pl.multiple_of(128 - mine, 128)

        def receive(step, carry):
            k, t = lax.div(step, GROUP), GROUP - 1 - lax.rem(step, GROUP)
            for n in range(2):
                landed(push_in.at[t, k, pl.ds(theirs + 64 * n, 64)], pass_got.at[t, k, n])
            keep(t, k, theirs)
            return carry

        lax.fori_loop(0, KMAX * GROUP, receive, 0)

        def receive_side(t, carry):
            landed(side_in.at[t], side_got.at[t])
            return carry

        lax.fori_loop(0, GROUP, receive_side, 0)

        def edge_copy(p, d):
            return pltpu.make_async_remote_copy(
                edge_out.at[p, d], edge_in.at[p, d], edge_sent.at[p, d], edge_got.at[p, d],
                device_id={"blk": next_b, "sims": s}, device_id_type=MESH,
            )

        @pl.when(is_first)
        def _():
            edge_out[...] = jnp.zeros_like(edge_out)
            for p in range(PIECES):
                for d in range(4):
                    pltpu.make_async_copy(edge_out.at[p, d], edge_in.at[p, d], edge_got.at[p, d]).start()

        def home(t):
            return 4 * (2 * half + lax.div(t, 4)) + lax.rem(t, 4)

        def is_home(t):
            return (part == 1) & (home(t) == b)

        def return_zeta(t, n):
            src = zeta.at[t, pl.ds(HALF * n, HALF)]
            dst = zeta_in.at[x, pl.ds(HALF * n, HALF)]

            @pl.when(is_home(t))
            def _():
                pltpu.make_async_copy(src, dst, zeta_got.at[x, n]).start()

            @pl.when(jnp.logical_not(is_home(t)))
            def _():
                pltpu.make_async_remote_copy(
                    src, dst, zeta_sent.at[t, n], zeta_got.at[x, n],
                    device_id={"blk": home(t), "sims": plane + part}, device_id_type=MESH,
                ).start()

        def piece(p, carry):
            here = pl.ds(pl.multiple_of(WIDTH * p, WIDTH), WIDTH)

            def far(t, both, high, pending):
                updates = []
                for k in (1, 2):
                    wide = dot(both, push_high[t, k])
                    updates.append(wide[:WIDTH] + (wide[WIDTH:] + dot(high, push_low[t, k])))
                for d in range(3):
                    first = side_in[t, COLS + d : COLS + d + 1, :] > 0.5
                    second = side_in[t, COLS + 3 + d : COLS + 4 + d, :] > 0.5
                    update = jnp.where(first, updates[0], jnp.where(second, updates[1], 0.0))
                    row = t - 2 - d
                    pending[row] = pending[row] + update if row in pending else update

            pending = {}
            for t in reversed(range(GROUP)):
                d = GROUP - 1 - t
                if d < 4:
                    landed(edge_in.at[p, d], edge_got.at[p, d])
                    edge = edge_in[p, d]
                    pending[t] = pending[t] + edge if t in pending else edge
                z = side_in[t, here, :] - pending[t]
                zeta[t, here, :] = z
                high, low = split(z)
                both = jnp.concatenate([high, low], 0)
                wide = dot(both, push_high[t, 0])
                low_part = dot(high, push_low[t, 0])
                update = wide[:WIDTH] + (wide[WIDTH:] + low_part)
                if t > 0:
                    far(t, both, high, pending)
                pending[t - 1] = pending[t - 1] + update if t - 1 in pending else update
            edge_out[p, 0] = pending[-1]

            @pl.when(jnp.logical_not(is_last))
            def _():
                edge_copy(p, 0).start()

            far(0, both, high, pending)
            for d in range(1, 4):
                edge_out[p, d] = pending[-1 - d]

            @pl.when(jnp.logical_not(is_last))
            def _():
                for d in range(1, 4):
                    edge_copy(p, d).start()

            @pl.when(lax.rem(p, PIECES // 2) == PIECES // 2 - 1)
            def _():
                def one(step, c):
                    return_zeta(GROUP - 1 - step, lax.div(p, PIECES // 2))
                    return c

                lax.fori_loop(0, GROUP, one, 0)

            return carry

        lax.fori_loop(0, early, finish_down, 0)
        lax.fori_loop(0, PIECES, piece, 0)

        @pl.when(x == 3)
        def _():
            share_weights()

        lax.fori_loop(early, ROWS, finish_down, 0)

        @pl.when(jnp.logical_not(is_last))
        def _():
            for p in range(PIECES):
                for d in range(4):
                    edge_copy(p, d).wait_send()

        def sent_one(step, c):
            t, n = lax.div(step, 2), lax.rem(step, 2)

            @pl.when(jnp.logical_not(is_home(t)))
            def _():
                landed(zeta.at[t, pl.ds(HALF * n, HALF)], zeta_sent.at[t, n])

            return c

        lax.fori_loop(0, 2 * GROUP, sent_one, 0)

        def passed(t, c):
            for k in range(KMAX):
                for n in range(2):
                    quarter(t, k, n).wait_send()
            return c

        lax.fori_loop(0, GROUP, passed, 0)

    exchange(numer, numer_in, numer_sent, numer_got)

    def sent_side(r, carry):
        sent(r, [(side_out.at[r], side_sent.at[r])])
        return carry

    lax.fori_loop(0, ROWS, sent_side, 0)
    exchanged(denom, denom_in, denom_sent, denom_got)
    exchanged(numer, numer_in, numer_sent, numer_got)
    mean_ref[...] = jnp.sum(numer_in[...], 0) / jnp.sum(denom_in[...], 0)


def body(rhs, lower_blocks, col_index, diag_inverse, turnout, district_of):
    vmem = pl.BlockSpec(memory_space=pltpu.VMEM)
    hbm = pl.BlockSpec(memory_space=pltpu.HBM)
    dma = pltpu.SemaphoreType.DMA
    field, mean = pl.pallas_call(
        kernel,
        out_shape=(
            jax.ShapeDtypeStruct((ROWS, BS, COLS), F32),
            jax.ShapeDtypeStruct((SHARE, COLS), F32),
        ),
        in_specs=[hbm, hbm, pl.BlockSpec(memory_space=pltpu.SMEM), hbm, vmem, vmem],
        out_specs=(vmem, vmem),
        scratch_shapes=[
            pltpu.VMEM((ROWS, BS, COLS), F32),
            pltpu.VMEM((ROWS, KMAX, BS, BS), F32),
            pltpu.VMEM((ROWS, BS, BS), F32),
            pltpu.VMEM((ROWS, BS, BS), BF16),
            pltpu.VMEM((ROWS, BS, BS), BF16),
            pltpu.VMEM((ROWS, KMAX, BS // 2, BS), F32),
            pltpu.VMEM((ROWS, COLS + 8, BS), F32),
            pltpu.VMEM((GROUP, KMAX, BS, BS), F32),
            pltpu.VMEM((GROUP, COLS + 8, BS), F32),
            pltpu.VMEM((GROUP, KMAX, BS, BS), BF16),
            pltpu.VMEM((GROUP, KMAX, BS, BS), BF16),
            pltpu.VMEM((GROUP, COLS, BS), F32),
            pltpu.VMEM((ROWS, COLS, BS), F32),
            pltpu.VMEM((PIECES, 4, WIDTH, BS), F32),
            pltpu.VMEM((PIECES, 4, WIDTH, BS), F32),
            pltpu.VMEM((NDIST, COLS), F32),
            pltpu.VMEM((NB, SHARE, COLS), F32),
            pltpu.VMEM((NDIST, COLS), F32),
            pltpu.VMEM((NB, SHARE, COLS), F32),
            dma((ROWS, 3)), dma((ROWS, KMAX)), dma((GROUP, KMAX)), dma((GROUP, KMAX, 2)), dma((GROUP, KMAX, 2)),
            dma((ROWS,)), dma((GROUP,)), dma((PIECES, 4)), dma((PIECES, 4)),
            dma((GROUP, 2)), dma((ROWS, 2)),
            dma((NB,)), dma((NB,)), dma((NB,)), dma((NB,)),
        ],
        name="back_substitution",
        compiler_params=pltpu.CompilerParams(
            collective_id=0, has_side_effects=True, vmem_limit_bytes=48 * 1024 * 1024
        ),
    )(
        in_hbm(rhs), in_hbm(lower_blocks), jnp.transpose(col_index, (2, 1, 0)), in_hbm(diag_inverse),
        turnout, district_of,
    )
    return field[:, None], mean


def solution(mesh):
    placed = (
        P(None, "blk", None, "sims"),
        P(None, "blk", None, None, None),
        P(None, "blk", None),
        P(None, "blk", None, None),
        P(None, "blk", None),
        P(None, "blk", None),
    )
    return jax.shard_map(
        body,
        mesh=mesh,
        in_specs=placed,
        out_specs=(P(None, "blk", None, "sims"), P("blk", "sims")),
        check_vma=False,
    )
```

```python
import jax
import jax.numpy as jnp
from jax import lax
from jax.experimental import pallas as pl
from jax.experimental.pallas import tpu as pltpu
from jax.sharding import PartitionSpec as P

MESH = pl.DeviceIdType.MESH
F32 = jnp.float32
BF16 = jnp.bfloat16

BS = 256
ROWS = 4
KMAX = 3
COLS = 128
NB = 16
NDIST = 256
SHARE = NDIST // NB
GROUP = 8
PIECES = 4
WIDTH = COLS // PIECES


def split(value):
    high = value.astype(BF16)
    return high, (value - high.astype(F32)).astype(BF16)


def dot(a, b):
    return jnp.dot(a, b, preferred_element_type=F32)


def landed(ref, sem):
    pltpu.make_async_copy(ref, ref, sem).wait()


def in_hbm(array):
    return pltpu.with_memory_space_constraint(array, pltpu.HBM)


def kernel(
    rhs_hbm, lower_hbm, col_ref, diag_hbm, turn_hbm, dist_hbm,
    sol_ref, mean_ref,
    rhs_ref, lower_ref, diag_ref, turn_ref, dist_ref,
    diag_high, diag_low, push_out, side_out, side_twin, push_in, side_in, push_high, push_low,
    zeta, zeta_in, edge_in, edge_out, numer, numer_in, denom, denom_in,
    read_got, small_got, push_sent, push_got, pass_sent, pass_got, twin_sent, twin_got, side_sent, side_got, edge_sent, edge_got,
    zeta_sent, zeta_got, numer_sent, numer_got, denom_sent, denom_got,
):
    b = lax.axis_index("blk")
    s = lax.axis_index("sims")
    y, x = lax.div(b, 4), lax.rem(b, 4)
    core = lax.rem(s, 2)
    plane = s - core
    z_here = lax.div(s, 2)
    mine = pl.multiple_of(128 * lax.rem(z_here, 2), 128)

    def reads(r):
        return (
            pltpu.make_async_copy(diag_hbm.at[r, 0], diag_ref.at[r], read_got.at[r, 0]),
            pltpu.make_async_copy(lower_hbm.at[r, 0], lower_ref.at[r], read_got.at[r, 1]),
            pltpu.make_async_copy(rhs_hbm.at[r, 0], rhs_ref.at[r], read_got.at[r, 2]),
        )

    def start_reads(step, carry):
        for copy in reads(3 - step):
            copy.start()
        return carry

    lax.fori_loop(0, ROWS, start_reads, 0)
    small = (
        pltpu.make_async_copy(turn_hbm, turn_ref, small_got.at[0]),
        pltpu.make_async_copy(dist_hbm, dist_ref, small_got.at[1]),
    )
    for copy in small:
        copy.start()

    barrier = pltpu.get_barrier_semaphore()

    def hail(other_blk, other_sims):
        pl.semaphore_signal(barrier, inc=1, device_id={"blk": other_blk, "sims": other_sims}, device_id_type=MESH)

    upper = lax.div(y, 2)
    lane = jnp.where(upper == 1, lax.rem(y, 2), 1 - lax.rem(y, 2))

    def greet(step, carry):
        hail(lax.rem(b + step, NB), s)
        return carry

    lax.fori_loop(1, NB, greet, 0)

    @pl.when(core == 0)
    def _():
        for r in range(ROWS):
            for there in (0, 1):
                hail(4 * jnp.where(upper == 1, 2 + there, 1 - there) + r, plane + 1)

    @pl.when(core == 1)
    def _():
        for t in range(GROUP):
            hail(8 * upper + t, plane)

    above = plane + core + 2 - 8 * lax.div(plane + 2, 8)
    below = lax.rem(plane + 6, 8) + core
    for other in (above, below):
        pl.semaphore_signal(barrier, inc=1, device_id={"blk": b, "sims": other}, device_id_type=MESH)

    upper = lax.div(y, 2)
    own_y = jnp.where(upper == 1, 2 + core, 1 - core)
    slot = 4 * lax.rem(y, 2) + x

    def prepare_side(r):
        for copy in reads(r):
            copy.wait()
        high, low = split(diag_ref[r])
        diag_high[r] = high
        diag_low[r] = low
        side_out[r, :COLS] = rhs_ref[r].T
        row = 16 * r + b
        masks = []
        for k in (1, 2):
            column = jnp.full((1, BS), col_ref[k, 0, r], jnp.int32)
            for d in (2, 3, 4):
                masks.append(jnp.where((column >= 0) & (column == row - d), 1.0, 0.0).astype(F32))
        masks.append(jnp.zeros((2, BS), F32))
        side_out[r, COLS:] = jnp.concatenate(masks, 0)

    def prepare(r, k):
        high, low = diag_high[r, pl.ds(mine, 128), :], diag_low[r, pl.ds(mine, 128), :]
        both = jnp.concatenate([high, low], 0)
        l_high, l_low = split(lower_ref[r, k])
        wide = dot(both, l_high)
        push_out[r, k] = wide[:128] + (wide[128:] + dot(high, l_low))

    def owner_of(r, there):
        return {"blk": 4 * jnp.where(upper == 1, 2 + there, 1 - there) + r, "sims": plane + 1}

    def twin_copy(r):
        return pltpu.make_async_remote_copy(
            side_out.at[r], side_twin.at[r], twin_sent.at[r], twin_got.at[r],
            device_id={"blk": b, "sims": plane}, device_id_type=MESH,
        )

    def side_copies(r):
        return [
            pltpu.make_async_remote_copy(
                (side_out, side_twin)[there].at[r], side_in.at[slot], side_sent.at[r, there], side_got.at[slot],
                device_id=owner_of(r, there), device_id_type=MESH,
            )
            for there in (0, 1)
        ]

    def send_side(r):
        landed(side_twin.at[r], twin_got.at[r])
        for copy in side_copies(r):
            copy.start()

    def push_copies(r, k):
        return [
            pltpu.make_async_remote_copy(
                push_out.at[r, k], push_in.at[slot, k, pl.ds(mine, 128)], push_sent.at[r, k, there], push_got.at[slot, k],
                device_id=owner_of(r, there), device_id_type=MESH,
            )
            for there in (0, 1)
        ]

    def quarter(t, k, n):
        where = push_in.at[t, k, pl.ds(mine + 64 * n, 64)]
        return pltpu.make_async_remote_copy(
            where, where, pass_sent.at[t, k, n], pass_got.at[t, k, n],
            device_id={"blk": b, "sims": (above, below)[n]}, device_id_type=MESH,
        )

    def keep(t, k, start):
        rows = pl.ds(start, 128)
        high, low = split(push_in[t, k, rows, :])
        push_high[t, k, rows, :] = high
        push_low[t, k, rows, :] = low

    def forward(step, carry):
        k, t = lax.div(step, GROUP), GROUP - 1 - lax.rem(step, GROUP)
        landed(push_in.at[t, k, pl.ds(mine, 128)], push_got.at[t, k])
        for n in range(2):
            quarter(t, k, n).start()
        keep(t, k, mine)
        return carry

    def receive_all(k):
        theirs = pl.multiple_of(128 - mine, 128)

        def one(step, carry):
            t = GROUP - 1 - step
            for n in range(2):
                landed(push_in.at[t, k, pl.ds(theirs + 64 * n, 64)], pass_got.at[t, k, n])
            keep(t, k, theirs)
            return carry

        lax.fori_loop(0, GROUP, one, 0)

    def forward_all(k):
        def one(step, carry):
            forward(k * GROUP + step, 0)
            return carry

        lax.fori_loop(0, GROUP, one, 0)

    def sent_push(k):
        def one(r, carry):
            for copy in push_copies(r, k):
                copy.wait_send()
            return carry

        lax.fori_loop(0, ROWS, one, 0)

    def push_all(k):
        def one(step, carry):
            r = 3 - step
            prepare(r, k)
            for copy in push_copies(r, k):
                copy.start()
            return carry

        lax.fori_loop(0, ROWS, one, 0)

    def prepare_sides(step, carry):
        prepare_side(3 - step)
        return carry

    lax.fori_loop(0, 1, prepare_sides, 0)

    @pl.when(core == 0)
    def _():
        prepare(3, 0)

    pl.semaphore_wait(barrier, NB + 1 + 2 * ROWS)

    @pl.when(core == 0)
    def _():
        for copy in push_copies(3, 0):
            copy.start()

    lax.fori_loop(1, ROWS, prepare_sides, 0)

    @pl.when(core == 0)
    def _():
        def first(step, carry):
            r = 2 - step
            prepare(r, 0)
            for copy in push_copies(r, 0):
                copy.start()
            return carry

        lax.fori_loop(0, 3, first, 0)
        push_all(1)
        push_all(2)
        send_side(3)
        for k in range(KMAX):
            sent_push(k)
        for r in (2, 1, 0):
            send_side(r)

    @pl.when(core == 1)
    def _():
        for r in range(ROWS):
            twin_copy(r).start()
        forward_all(0)
        forward_all(1)
        receive_all(0)
        forward_all(2)
        receive_all(1)
        receive_all(2)

    for copy in small:
        copy.wait()

    def members(r):
        ids = dist_ref[r]
        return lax.broadcasted_iota(jnp.int32, (NDIST, BS), 0) == ids

    numer[...] = jnp.zeros_like(numer)

    def exchange(source, target, sent, got):
        def one(step, carry):
            other = lax.rem(b + step, NB)
            pltpu.make_async_remote_copy(
                source.at[pl.ds(SHARE * other, SHARE)], target.at[b], sent.at[other], got.at[b],
                device_id={"blk": other, "sims": s}, device_id_type=MESH,
            ).start()
            return carry

        lax.fori_loop(1, NB, one, 0, unroll=True)
        target[b] = source[pl.ds(pl.multiple_of(SHARE * b, SHARE), SHARE), :]

    def exchanged(source, target, sent, got):
        def one(step, carry):
            other = lax.rem(b + step, NB)
            landed(target.at[other], got.at[other])
            landed(source.at[pl.ds(SHARE * other, SHARE)], sent.at[other])
            return carry

        lax.fori_loop(1, NB, one, 0, unroll=True)

    def share_weights():
        weight = jnp.zeros((NDIST, BS), F32)
        for r in range(ROWS):
            weight = weight + jnp.where(members(r), turn_ref[r], 0.0)
        denom[...] = jnp.broadcast_to(jnp.sum(weight, 1, keepdims=True), (NDIST, COLS))
        exchange(denom, denom_in, denom_sent, denom_got)

    @pl.when((core == 0) | (x < 3))
    def _():
        share_weights()

    def finish(r):
        landed(zeta_in.at[r], zeta_got.at[r])
        high, low = split(zeta_in[r])
        both = jnp.concatenate([high, low], 0)
        wide = dot(both, diag_high[r])
        field = wide[:COLS] + (wide[COLS:] + dot(high, diag_low[r]))
        sol_ref[r] = field.T
        w_high, w_low = split(field * turn_ref[r])
        member = jnp.where(members(r), 1.0, 0.0).astype(BF16)
        contract = (((1,), (1,)), ((), ()))
        numer[...] += lax.dot_general(
            member, w_high, contract, preferred_element_type=F32
        ) + lax.dot_general(member, w_low, contract, preferred_element_type=F32)

    def finish_down(step, carry):
        finish(3 - step)
        return carry

    @pl.when(core == 0)
    def _():
        lax.fori_loop(0, ROWS, finish_down, 0)

    @pl.when(core == 1)
    def _():
        half = lax.div(y, 2)
        part = jnp.where(half == 1, lax.rem(y, 2), 1 - lax.rem(y, 2))
        is_first = (half == 1) & (x == 3)
        is_last = (half == 0) & (x == 0)
        next_b = jnp.where(half == 1, 4 * (1 - part) + x, 4 * (2 + part) + x - 1)

        early = jnp.maximum(2 - x, 0)
        def receive_side(t, carry):
            landed(side_in.at[t], side_got.at[t])
            return carry

        lax.fori_loop(0, GROUP, receive_side, 0)

        def edge_copy(p, d):
            return pltpu.make_async_remote_copy(
                edge_out.at[p, d], edge_in.at[p, d], edge_sent.at[p, d], edge_got.at[p, d],
                device_id={"blk": next_b, "sims": s}, device_id_type=MESH,
            )

        @pl.when(is_first)
        def _():
            edge_out[...] = jnp.zeros_like(edge_out)
            for p in range(PIECES):
                for d in range(4):
                    pltpu.make_async_copy(edge_out.at[p, d], edge_in.at[p, d], edge_got.at[p, d]).start()

        def home(t):
            return 4 * (2 * half + lax.div(t, 4)) + lax.rem(t, 4)

        def is_home(t):
            return (part == 1) & (home(t) == b)

        def return_zeta(rows):
            def one(step, carry):
                t = GROUP - 1 - step
                src, dst = zeta.at[t, rows], zeta_in.at[x, rows]

                @pl.when(is_home(t))
                def _():
                    pltpu.make_async_copy(src, dst, zeta_got.at[x]).start()

                @pl.when(jnp.logical_not(is_home(t)))
                def _():
                    pltpu.make_async_remote_copy(
                        src, dst, zeta_sent.at[t], zeta_got.at[x],
                        device_id={"blk": home(t), "sims": plane + part}, device_id_type=MESH,
                    ).start()

                return carry

            lax.fori_loop(0, GROUP, one, 0)

        def piece(p, carry):
            here = pl.ds(pl.multiple_of(WIDTH * p, WIDTH), WIDTH)

            def far(t, both, high, pending):
                updates = []
                for k in (1, 2):
                    wide = dot(both, push_high[t, k])
                    updates.append(wide[:WIDTH] + (wide[WIDTH:] + dot(high, push_low[t, k])))
                for d in range(3):
                    first = side_in[t, COLS + d : COLS + d + 1, :] > 0.5
                    second = side_in[t, COLS + 3 + d : COLS + 4 + d, :] > 0.5
                    update = jnp.where(first, updates[0], jnp.where(second, updates[1], 0.0))
                    row = t - 2 - d
                    pending[row] = pending[row] + update if row in pending else update

            pending = {}
            for t in reversed(range(GROUP)):
                d = GROUP - 1 - t
                if d < 4:
                    landed(edge_in.at[p, d], edge_got.at[p, d])
                    edge = edge_in[p, d]
                    pending[t] = pending[t] + edge if t in pending else edge
                z = side_in[t, here, :] - pending[t]
                zeta[t, here, :] = z
                high, low = split(z)
                both = jnp.concatenate([high, low], 0)
                wide = dot(both, push_high[t, 0])
                low_part = dot(high, push_low[t, 0])
                update = wide[:WIDTH] + (wide[WIDTH:] + low_part)
                far(t, both, high, pending)
                pending[t - 1] = pending[t - 1] + update if t - 1 in pending else update
            edge_out[p, 0] = pending[-1]

            @pl.when(jnp.logical_not(is_last))
            def _():
                edge_copy(p, 0).start()

            for d in range(1, 4):
                edge_out[p, d] = pending[-1 - d]

            @pl.when(jnp.logical_not(is_last))
            def _():
                for d in range(1, 4):
                    edge_copy(p, d).start()

            @pl.when(is_last)
            def _():
                return_zeta(here)

            return carry

        lax.fori_loop(0, early, finish_down, 0)
        lax.fori_loop(0, PIECES, piece, 0)

        @pl.when(jnp.logical_not(is_last))
        def _():
            return_zeta(pl.ds(0, COLS))


        @pl.when(x == 3)
        def _():
            share_weights()

        lax.fori_loop(early, ROWS, finish_down, 0)

        @pl.when(jnp.logical_not(is_last))
        def _():
            for p in range(PIECES):
                for d in range(4):
                    edge_copy(p, d).wait_send()

        def sent_one(t, c):
            @pl.when(jnp.logical_not(is_home(t)))
            def _():
                landed(zeta.at[t], zeta_sent.at[t])

            return c

        lax.fori_loop(0, GROUP, sent_one, 0)

        def passed(t, c):
            for k in range(KMAX):
                for n in range(2):
                    quarter(t, k, n).wait_send()
            return c

        lax.fori_loop(0, GROUP, passed, 0)

    exchange(numer, numer_in, numer_sent, numer_got)

    @pl.when(core == 0)
    def _():
        def sent_side(r, carry):
            for copy in side_copies(r):
                copy.wait_send()
            return carry

        lax.fori_loop(0, ROWS, sent_side, 0)

    @pl.when(core == 1)
    def _():
        def sent_twin(r, carry):
            twin_copy(r).wait_send()
            return carry

        lax.fori_loop(0, ROWS, sent_twin, 0)

    exchanged(denom, denom_in, denom_sent, denom_got)
    exchanged(numer, numer_in, numer_sent, numer_got)
    mean_ref[...] = jnp.sum(numer_in[...], 0) / jnp.sum(denom_in[...], 0)


def body(rhs, lower_blocks, col_index, diag_inverse, turnout, district_of):
    vmem = pl.BlockSpec(memory_space=pltpu.VMEM)
    hbm = pl.BlockSpec(memory_space=pltpu.HBM)
    dma = pltpu.SemaphoreType.DMA
    field, mean = pl.pallas_call(
        kernel,
        out_shape=(
            jax.ShapeDtypeStruct((ROWS, BS, COLS), F32),
            jax.ShapeDtypeStruct((SHARE, COLS), F32),
        ),
        in_specs=[hbm, hbm, pl.BlockSpec(memory_space=pltpu.SMEM), hbm, hbm, hbm],
        out_specs=(vmem, vmem),
        scratch_shapes=[
            pltpu.VMEM((ROWS, BS, COLS), F32),
            pltpu.VMEM((ROWS, KMAX, BS, BS), F32),
            pltpu.VMEM((ROWS, BS, BS), F32),
            pltpu.VMEM((ROWS, 1, BS), F32),
            pltpu.VMEM((ROWS, 1, BS), jnp.int32),
            pltpu.VMEM((ROWS, BS, BS), BF16),
            pltpu.VMEM((ROWS, BS, BS), BF16),
            pltpu.VMEM((ROWS, KMAX, BS // 2, BS), F32),
            pltpu.VMEM((ROWS, COLS + 8, BS), F32),
            pltpu.VMEM((ROWS, COLS + 8, BS), F32),
            pltpu.VMEM((GROUP, KMAX, BS, BS), F32),
            pltpu.VMEM((GROUP, COLS + 8, BS), F32),
            pltpu.VMEM((GROUP, KMAX, BS, BS), BF16),
            pltpu.VMEM((GROUP, KMAX, BS, BS), BF16),
            pltpu.VMEM((GROUP, COLS, BS), F32),
            pltpu.VMEM((ROWS, COLS, BS), F32),
            pltpu.VMEM((PIECES, 4, WIDTH, BS), F32),
            pltpu.VMEM((PIECES, 4, WIDTH, BS), F32),
            pltpu.VMEM((NDIST, COLS), F32),
            pltpu.VMEM((NB, SHARE, COLS), F32),
            pltpu.VMEM((NDIST, COLS), F32),
            pltpu.VMEM((NB, SHARE, COLS), F32),
            dma((ROWS, 3)), dma((2,)), dma((ROWS, KMAX, 2)), dma((GROUP, KMAX)), dma((GROUP, KMAX, 2)), dma((GROUP, KMAX, 2)),
            dma((ROWS,)), dma((ROWS,)), dma((ROWS, 2)), dma((GROUP,)), dma((PIECES, 4)), dma((PIECES, 4)),
            dma((GROUP,)), dma((ROWS,)),
            dma((NB,)), dma((NB,)), dma((NB,)), dma((NB,)),
        ],
        name="back_substitution",
        compiler_params=pltpu.CompilerParams(
            collective_id=0, has_side_effects=True, vmem_limit_bytes=48 * 1024 * 1024
        ),
    )(
        in_hbm(rhs), in_hbm(lower_blocks), jnp.transpose(col_index, (2, 1, 0)), in_hbm(diag_inverse),
        in_hbm(turnout), in_hbm(district_of),
    )
    return field[:, None], mean


def solution(mesh):
    placed = (
        P(None, "blk", None, "sims"),
        P(None, "blk", None, None, None),
        P(None, "blk", None),
        P(None, "blk", None, None),
        P(None, "blk", None),
        P(None, "blk", None),
    )
    return jax.shard_map(
        body,
        mesh=mesh,
        in_specs=placed,
        out_specs=(P(None, "blk", None, "sims"), P("blk", "sims")),
        check_vma=False,
    )
```

```python
import jax
import jax.numpy as jnp
from jax import lax
from jax.experimental import pallas as pl
from jax.experimental.pallas import tpu as pltpu
from jax.sharding import PartitionSpec as P

MESH = pl.DeviceIdType.MESH
F32 = jnp.float32
BF16 = jnp.bfloat16

BS = 256
ROWS = 4
KMAX = 3
COLS = 128
NB = 16
NDIST = 256
SHARE = NDIST // NB
GROUP = 8
PIECES = 4
WIDTH = COLS // PIECES


def split(value):
    high = value.astype(BF16)
    return high, (value - high.astype(F32)).astype(BF16)


def dot(a, b):
    return jnp.dot(a, b, preferred_element_type=F32)


def landed(ref, sem):
    pltpu.make_async_copy(ref, ref, sem).wait()


def in_hbm(array):
    return pltpu.with_memory_space_constraint(array, pltpu.HBM)


def kernel(
    rhs_hbm, lower_hbm, col_ref, diag_hbm, turn_hbm, dist_hbm,
    sol_ref, mean_ref,
    rhs_ref, lower_ref, diag_ref, turn_ref, dist_ref,
    diag_high, diag_low, push_out, side_out, side_twin, push_in, side_in, push_high, push_low,
    zeta, zeta_in, edge_in, edge_out, numer, numer_in, denom, denom_in,
    read_got, small_got, push_sent, push_got, pass_sent, pass_got, twin_sent, twin_got, side_sent, side_got, edge_sent, edge_got,
    zeta_sent, zeta_got, numer_sent, numer_got, denom_sent, denom_got,
):
    b = lax.axis_index("blk")
    s = lax.axis_index("sims")
    y, x = lax.div(b, 4), lax.rem(b, 4)
    core = lax.rem(s, 2)
    plane = s - core
    z_here = lax.div(s, 2)
    mine = pl.multiple_of(128 * lax.rem(z_here, 2), 128)

    def reads(r):
        return (
            pltpu.make_async_copy(diag_hbm.at[r, 0], diag_ref.at[r], read_got.at[r, 0]),
            pltpu.make_async_copy(lower_hbm.at[r, 0], lower_ref.at[r], read_got.at[r, 1]),
            pltpu.make_async_copy(rhs_hbm.at[r, 0], rhs_ref.at[r], read_got.at[r, 2]),
        )

    def start_reads(step, carry):
        for copy in reads(3 - step):
            copy.start()
        return carry

    lax.fori_loop(0, ROWS, start_reads, 0)
    small = (
        pltpu.make_async_copy(turn_hbm, turn_ref, small_got.at[0]),
        pltpu.make_async_copy(dist_hbm, dist_ref, small_got.at[1]),
    )
    for copy in small:
        copy.start()

    barrier = pltpu.get_barrier_semaphore()

    def hail(other_blk, other_sims):
        pl.semaphore_signal(barrier, inc=1, device_id={"blk": other_blk, "sims": other_sims}, device_id_type=MESH)

    upper = lax.div(y, 2)
    lane = jnp.where(upper == 1, lax.rem(y, 2), 1 - lax.rem(y, 2))

    def greet(step, carry):
        hail(lax.rem(b + step, NB), s)
        return carry

    lax.fori_loop(1, NB, greet, 0)

    @pl.when(core == 0)
    def _():
        for r in range(ROWS):
            for there in (0, 1):
                hail(4 * jnp.where(upper == 1, 2 + there, 1 - there) + r, plane + 1)

    @pl.when(core == 1)
    def _():
        for t in range(GROUP):
            hail(8 * upper + t, plane)

    above = plane + core + 2 - 8 * lax.div(plane + 2, 8)
    below = lax.rem(plane + 6, 8) + core
    for other in (above, below):
        pl.semaphore_signal(barrier, inc=1, device_id={"blk": b, "sims": other}, device_id_type=MESH)

    upper = lax.div(y, 2)
    own_y = jnp.where(upper == 1, 2 + core, 1 - core)
    slot = 4 * lax.rem(y, 2) + x

    def prepare_side(r):
        for copy in reads(r):
            copy.wait()
        high, low = split(diag_ref[r])
        diag_high[r] = high
        diag_low[r] = low
        side_out[r, :COLS] = rhs_ref[r].T
        row = 16 * r + b
        masks = []
        for k in (1, 2):
            column = jnp.full((1, BS), col_ref[k, 0, r], jnp.int32)
            for d in (2, 3, 4):
                masks.append(jnp.where((column >= 0) & (column == row - d), 1.0, 0.0).astype(F32))
        masks.append(jnp.zeros((2, BS), F32))
        side_out[r, COLS:] = jnp.concatenate(masks, 0)

    def prepare(r, k):
        high, low = diag_high[r, pl.ds(mine, 128), :], diag_low[r, pl.ds(mine, 128), :]
        both = jnp.concatenate([high, low], 0)
        l_high, l_low = split(lower_ref[r, k])
        wide = dot(both, l_high)
        push_out[r, k] = wide[:128] + (wide[128:] + dot(high, l_low))

    def owner_of(r, there):
        return {"blk": 4 * jnp.where(upper == 1, 2 + there, 1 - there) + r, "sims": plane + 1}

    def twin_copy(r):
        return pltpu.make_async_remote_copy(
            side_out.at[r], side_twin.at[r], twin_sent.at[r], twin_got.at[r],
            device_id={"blk": b, "sims": plane}, device_id_type=MESH,
        )

    def side_copies(r):
        return [
            pltpu.make_async_remote_copy(
                (side_out, side_twin)[there].at[r], side_in.at[slot], side_sent.at[r, there], side_got.at[slot],
                device_id=owner_of(r, there), device_id_type=MESH,
            )
            for there in (0, 1)
        ]

    def send_side(r):
        landed(side_twin.at[r], twin_got.at[r])
        for copy in side_copies(r):
            copy.start()

    def push_copies(r, k):
        return [
            pltpu.make_async_remote_copy(
                push_out.at[r, k], push_in.at[slot, k, pl.ds(mine, 128)], push_sent.at[r, k, there], push_got.at[slot, k],
                device_id=owner_of(r, there), device_id_type=MESH,
            )
            for there in (0, 1)
        ]

    def quarter(t, k, n):
        where = push_in.at[t, k, pl.ds(mine + 64 * n, 64)]
        return pltpu.make_async_remote_copy(
            where, where, pass_sent.at[t, k, n], pass_got.at[t, k, n],
            device_id={"blk": b, "sims": (above, below)[n]}, device_id_type=MESH,
        )

    def keep(t, k, start):
        rows = pl.ds(start, 128)
        high, low = split(push_in[t, k, rows, :])
        push_high[t, k, rows, :] = high
        push_low[t, k, rows, :] = low

    def forward(step, carry):
        k, t = lax.div(step, GROUP), GROUP - 1 - lax.rem(step, GROUP)
        landed(push_in.at[t, k, pl.ds(mine, 128)], push_got.at[t, k])
        for n in range(2):
            quarter(t, k, n).start()
        keep(t, k, mine)
        return carry

    def receive_all(k):
        theirs = pl.multiple_of(128 - mine, 128)

        def one(step, carry):
            t = GROUP - 1 - step
            for n in range(2):
                landed(push_in.at[t, k, pl.ds(theirs + 64 * n, 64)], pass_got.at[t, k, n])
            keep(t, k, theirs)
            return carry

        lax.fori_loop(0, GROUP, one, 0)

    def forward_all(k):
        def one(step, carry):
            forward(k * GROUP + step, 0)
            return carry

        lax.fori_loop(0, GROUP, one, 0)

    def sent_push(k):
        def one(r, carry):
            for copy in push_copies(r, k):
                copy.wait_send()
            return carry

        lax.fori_loop(0, ROWS, one, 0)

    def push_all(k):
        def one(step, carry):
            r = 3 - step
            prepare(r, k)
            for copy in push_copies(r, k):
                copy.start()
            return carry

        lax.fori_loop(0, ROWS, one, 0)

    def prepare_sides(step, carry):
        prepare_side(3 - step)
        return carry

    lax.fori_loop(0, 1, prepare_sides, 0)

    @pl.when(core == 0)
    def _():
        prepare(3, 0)

    pl.semaphore_wait(barrier, NB + 1 + 2 * ROWS)

    @pl.when(core == 0)
    def _():
        for copy in push_copies(3, 0):
            copy.start()

    lax.fori_loop(1, ROWS, prepare_sides, 0)

    @pl.when(core == 0)
    def _():
        def first(step, carry):
            r = 2 - step
            prepare(r, 0)
            for copy in push_copies(r, 0):
                copy.start()
            return carry

        lax.fori_loop(0, 3, first, 0)
        push_all(1)
        push_all(2)
        send_side(3)
        for k in range(KMAX):
            sent_push(k)
        for r in (2, 1, 0):
            send_side(r)

    @pl.when(core == 1)
    def _():
        @pl.when((upper == 1) & (x == 3))
        def _():
            edge_out[...] = jnp.zeros_like(edge_out)
            for p in range(PIECES):
                for d in range(4):
                    pltpu.make_async_copy(edge_out.at[p, d], edge_in.at[p, d], edge_got.at[p, d]).start()

        for r in range(ROWS):
            twin_copy(r).start()
        forward_all(0)
        forward_all(1)
        receive_all(0)
        forward_all(2)
        receive_all(1)
        receive_all(2)

    for copy in small:
        copy.wait()

    def members(r):
        ids = dist_ref[r]
        return lax.broadcasted_iota(jnp.int32, (NDIST, BS), 0) == ids

    numer[...] = jnp.zeros_like(numer)

    def exchange(source, target, sent, got):
        def one(step, carry):
            other = lax.rem(b + step, NB)
            pltpu.make_async_remote_copy(
                source.at[pl.ds(SHARE * other, SHARE)], target.at[b], sent.at[other], got.at[b],
                device_id={"blk": other, "sims": s}, device_id_type=MESH,
            ).start()
            return carry

        lax.fori_loop(1, NB, one, 0, unroll=True)
        target[b] = source[pl.ds(pl.multiple_of(SHARE * b, SHARE), SHARE), :]

    def exchanged(source, target, sent, got):
        def one(step, carry):
            other = lax.rem(b + step, NB)
            landed(target.at[other], got.at[other])
            landed(source.at[pl.ds(SHARE * other, SHARE)], sent.at[other])
            return carry

        lax.fori_loop(1, NB, one, 0, unroll=True)

    def share_weights():
        weight = jnp.zeros((NDIST, BS), F32)
        for r in range(ROWS):
            weight = weight + jnp.where(members(r), turn_ref[r], 0.0)
        denom[...] = jnp.broadcast_to(jnp.sum(weight, 1, keepdims=True), (NDIST, COLS))
        exchange(denom, denom_in, denom_sent, denom_got)

    @pl.when((core == 0) | (x < 3))
    def _():
        share_weights()

    def finish(r):
        landed(zeta_in.at[r], zeta_got.at[r])
        high, low = split(zeta_in[r])
        both = jnp.concatenate([high, low], 0)
        wide = dot(both, diag_high[r])
        field = wide[:COLS] + (wide[COLS:] + dot(high, diag_low[r]))
        sol_ref[r] = field.T
        w_high, w_low = split(field * turn_ref[r])
        member = jnp.where(members(r), 1.0, 0.0).astype(BF16)
        contract = (((1,), (1,)), ((), ()))
        numer[...] += lax.dot_general(
            member, w_high, contract, preferred_element_type=F32
        ) + lax.dot_general(member, w_low, contract, preferred_element_type=F32)

    def finish_down(step, carry):
        finish(3 - step)
        return carry

    @pl.when(core == 0)
    def _():
        lax.fori_loop(0, ROWS, finish_down, 0)

    @pl.when(core == 1)
    def _():
        half = lax.div(y, 2)
        part = jnp.where(half == 1, lax.rem(y, 2), 1 - lax.rem(y, 2))
        is_last = (half == 0) & (x == 0)
        next_b = jnp.where(half == 1, 4 * (1 - part) + x, 4 * (2 + part) + x - 1)

        early = jnp.maximum(2 - x, 0)
        def receive_side(t, carry):
            landed(side_in.at[t], side_got.at[t])
            return carry

        lax.fori_loop(0, GROUP, receive_side, 0)

        def edge_copy(p, d):
            return pltpu.make_async_remote_copy(
                edge_out.at[p, d], edge_in.at[p, d], edge_sent.at[p, d], edge_got.at[p, d],
                device_id={"blk": next_b, "sims": s}, device_id_type=MESH,
            )

        def home(t):
            return 4 * (2 * half + lax.div(t, 4)) + lax.rem(t, 4)

        def is_home(t):
            return (part == 1) & (home(t) == b)

        def return_zeta(rows):
            def one(step, carry):
                t = GROUP - 1 - step
                src, dst = zeta.at[t, rows], zeta_in.at[x, rows]

                @pl.when(is_home(t))
                def _():
                    pltpu.make_async_copy(src, dst, zeta_got.at[x]).start()

                @pl.when(jnp.logical_not(is_home(t)))
                def _():
                    pltpu.make_async_remote_copy(
                        src, dst, zeta_sent.at[t], zeta_got.at[x],
                        device_id={"blk": home(t), "sims": plane + part}, device_id_type=MESH,
                    ).start()

                return carry

            lax.fori_loop(0, GROUP, one, 0)

        def piece(p, carry):
            here = pl.ds(pl.multiple_of(WIDTH * p, WIDTH), WIDTH)

            def far(t, both, high, pending):
                updates = []
                for k in (1, 2):
                    wide = dot(both, push_high[t, k])
                    updates.append(wide[:WIDTH] + (wide[WIDTH:] + dot(high, push_low[t, k])))
                for d in range(3):
                    first = side_in[t, COLS + d : COLS + d + 1, :] > 0.5
                    second = side_in[t, COLS + 3 + d : COLS + 4 + d, :] > 0.5
                    update = jnp.where(first, updates[0], jnp.where(second, updates[1], 0.0))
                    row = t - 2 - d
                    pending[row] = pending[row] + update if row in pending else update

            pending = {}
            for t in reversed(range(GROUP)):
                d = GROUP - 1 - t
                if d < 4:
                    landed(edge_in.at[p, d], edge_got.at[p, d])
                    edge = edge_in[p, d]
                    pending[t] = pending[t] + edge if t in pending else edge
                z = side_in[t, here, :] - pending[t]
                zeta[t, here, :] = z
                high, low = split(z)
                both = jnp.concatenate([high, low], 0)
                wide = dot(both, push_high[t, 0])
                low_part = dot(high, push_low[t, 0])
                update = wide[:WIDTH] + (wide[WIDTH:] + low_part)
                far(t, both, high, pending)
                pending[t - 1] = pending[t - 1] + update if t - 1 in pending else update
            edge_out[p, 0] = pending[-1]

            @pl.when(jnp.logical_not(is_last))
            def _():
                edge_copy(p, 0).start()

            for d in range(1, 4):
                edge_out[p, d] = pending[-1 - d]

            @pl.when(jnp.logical_not(is_last))
            def _():
                for d in range(1, 4):
                    edge_copy(p, d).start()

            @pl.when(is_last)
            def _():
                return_zeta(here)

            return carry

        lax.fori_loop(0, early, finish_down, 0)
        lax.fori_loop(0, PIECES, piece, 0)

        @pl.when(jnp.logical_not(is_last))
        def _():
            return_zeta(pl.ds(0, COLS))


        @pl.when(x == 3)
        def _():
            share_weights()

        lax.fori_loop(early, ROWS, finish_down, 0)

        @pl.when(jnp.logical_not(is_last))
        def _():
            for p in range(PIECES):
                for d in range(4):
                    edge_copy(p, d).wait_send()

        def sent_one(t, c):
            @pl.when(jnp.logical_not(is_home(t)))
            def _():
                landed(zeta.at[t], zeta_sent.at[t])

            return c

        lax.fori_loop(0, GROUP, sent_one, 0)

        def passed(t, c):
            for k in range(KMAX):
                for n in range(2):
                    quarter(t, k, n).wait_send()
            return c

        lax.fori_loop(0, GROUP, passed, 0)

    exchange(numer, numer_in, numer_sent, numer_got)

    @pl.when(core == 0)
    def _():
        def sent_side(r, carry):
            for copy in side_copies(r):
                copy.wait_send()
            return carry

        lax.fori_loop(0, ROWS, sent_side, 0)

    @pl.when(core == 1)
    def _():
        def sent_twin(r, carry):
            twin_copy(r).wait_send()
            return carry

        lax.fori_loop(0, ROWS, sent_twin, 0)

    exchanged(denom, denom_in, denom_sent, denom_got)
    exchanged(numer, numer_in, numer_sent, numer_got)
    mean_ref[...] = jnp.sum(numer_in[...], 0) / jnp.sum(denom_in[...], 0)


def body(rhs, lower_blocks, col_index, diag_inverse, turnout, district_of):
    vmem = pl.BlockSpec(memory_space=pltpu.VMEM)
    hbm = pl.BlockSpec(memory_space=pltpu.HBM)
    dma = pltpu.SemaphoreType.DMA
    field, mean = pl.pallas_call(
        kernel,
        out_shape=(
            jax.ShapeDtypeStruct((ROWS, BS, COLS), F32),
            jax.ShapeDtypeStruct((SHARE, COLS), F32),
        ),
        in_specs=[hbm, hbm, pl.BlockSpec(memory_space=pltpu.SMEM), hbm, hbm, hbm],
        out_specs=(vmem, vmem),
        scratch_shapes=[
            pltpu.VMEM((ROWS, BS, COLS), F32),
            pltpu.VMEM((ROWS, KMAX, BS, BS), F32),
            pltpu.VMEM((ROWS, BS, BS), F32),
            pltpu.VMEM((ROWS, 1, BS), F32),
            pltpu.VMEM((ROWS, 1, BS), jnp.int32),
            pltpu.VMEM((ROWS, BS, BS), BF16),
            pltpu.VMEM((ROWS, BS, BS), BF16),
            pltpu.VMEM((ROWS, KMAX, BS // 2, BS), F32),
            pltpu.VMEM((ROWS, COLS + 8, BS), F32),
            pltpu.VMEM((ROWS, COLS + 8, BS), F32),
            pltpu.VMEM((GROUP, KMAX, BS, BS), F32),
            pltpu.VMEM((GROUP, COLS + 8, BS), F32),
            pltpu.VMEM((GROUP, KMAX, BS, BS), BF16),
            pltpu.VMEM((GROUP, KMAX, BS, BS), BF16),
            pltpu.VMEM((GROUP, COLS, BS), F32),
            pltpu.VMEM((ROWS, COLS, BS), F32),
            pltpu.VMEM((PIECES, 4, WIDTH, BS), F32),
            pltpu.VMEM((PIECES, 4, WIDTH, BS), F32),
            pltpu.VMEM((NDIST, COLS), F32),
            pltpu.VMEM((NB, SHARE, COLS), F32),
            pltpu.VMEM((NDIST, COLS), F32),
            pltpu.VMEM((NB, SHARE, COLS), F32),
            dma((ROWS, 3)), dma((2,)), dma((ROWS, KMAX, 2)), dma((GROUP, KMAX)), dma((GROUP, KMAX, 2)), dma((GROUP, KMAX, 2)),
            dma((ROWS,)), dma((ROWS,)), dma((ROWS, 2)), dma((GROUP,)), dma((PIECES, 4)), dma((PIECES, 4)),
            dma((GROUP,)), dma((ROWS,)),
            dma((NB,)), dma((NB,)), dma((NB,)), dma((NB,)),
        ],
        name="back_substitution",
        compiler_params=pltpu.CompilerParams(
            collective_id=0, has_side_effects=True, vmem_limit_bytes=48 * 1024 * 1024
        ),
    )(
        in_hbm(rhs), in_hbm(lower_blocks), jnp.transpose(col_index, (2, 1, 0)), in_hbm(diag_inverse),
        in_hbm(turnout), in_hbm(district_of),
    )
    return field[:, None], mean


def solution(mesh):
    placed = (
        P(None, "blk", None, "sims"),
        P(None, "blk", None, None, None),
        P(None, "blk", None),
        P(None, "blk", None, None),
        P(None, "blk", None),
        P(None, "blk", None),
    )
    return jax.shard_map(
        body,
        mesh=mesh,
        in_specs=placed,
        out_specs=(P(None, "blk", None, "sims"), P("blk", "sims")),
        check_vma=False,
    )
```

```python
import jax
import jax.numpy as jnp
from jax import lax
from jax.experimental import pallas as pl
from jax.experimental.pallas import tpu as pltpu
from jax.sharding import PartitionSpec as P

MESH = pl.DeviceIdType.MESH
F32 = jnp.float32
BF16 = jnp.bfloat16

BS = 256
ROWS = 4
KMAX = 3
COLS = 128
NB = 16
NDIST = 256
SHARE = NDIST // NB
GROUP = 8
PIECES = 4
WIDTH = COLS // PIECES


def split(value):
    high = value.astype(BF16)
    return high, (value - high.astype(F32)).astype(BF16)


def dot(a, b):
    return jnp.dot(a, b, preferred_element_type=F32)


def landed(ref, sem):
    pltpu.make_async_copy(ref, ref, sem).wait()


def in_hbm(array):
    return pltpu.with_memory_space_constraint(array, pltpu.HBM)


def kernel(
    rhs_hbm, lower_hbm, col_hbm, diag_hbm, turn_hbm, dist_hbm,
    sol_ref, mean_ref,
    rhs_ref, lower_ref, diag_ref, turn_ref, dist_ref, col_ref,
    diag_high, diag_low, push_out, side_out, side_twin, push_in, side_in, push_high, push_low,
    zeta, zeta_in, edge_in, edge_out, numer, numer_in, denom, denom_in,
    read_got, small_got, push_sent, push_got, pass_sent, pass_got, twin_sent, twin_got, side_sent, side_got, edge_sent, edge_got,
    zeta_sent, zeta_got, numer_sent, numer_got, denom_sent, denom_got,
):
    b = lax.axis_index("blk")
    s = lax.axis_index("sims")
    y, x = lax.div(b, 4), lax.rem(b, 4)
    core = lax.rem(s, 2)
    plane = s - core
    z_here = lax.div(s, 2)
    mine = pl.multiple_of(128 * lax.rem(z_here, 2), 128)

    def reads(r):
        return (
            pltpu.make_async_copy(diag_hbm.at[r, 0], diag_ref.at[r], read_got.at[r, 0]),
            pltpu.make_async_copy(lower_hbm.at[r, 0], lower_ref.at[r], read_got.at[r, 1]),
            pltpu.make_async_copy(rhs_hbm.at[r, 0], rhs_ref.at[r], read_got.at[r, 2]),
        )

    def start_reads(step, carry):
        for copy in reads(3 - step):
            copy.start()
        return carry

    columns = pltpu.make_async_copy(col_hbm, col_ref, small_got.at[2])
    columns.start()
    lax.fori_loop(0, ROWS, start_reads, 0)
    small = (
        pltpu.make_async_copy(turn_hbm, turn_ref, small_got.at[0]),
        pltpu.make_async_copy(dist_hbm, dist_ref, small_got.at[1]),
    )
    for copy in small:
        copy.start()

    barrier = pltpu.get_barrier_semaphore()

    def hail(other_blk, other_sims):
        pl.semaphore_signal(barrier, inc=1, device_id={"blk": other_blk, "sims": other_sims}, device_id_type=MESH)

    upper = lax.div(y, 2)
    lane = jnp.where(upper == 1, lax.rem(y, 2), 1 - lax.rem(y, 2))

    def greet(step, carry):
        hail(lax.rem(b + step, NB), s)
        return carry

    lax.fori_loop(1, NB, greet, 0)

    @pl.when(core == 0)
    def _():
        for r in range(ROWS):
            for there in (0, 1):
                hail(4 * jnp.where(upper == 1, 2 + there, 1 - there) + r, plane + 1)

    @pl.when(core == 1)
    def _():
        for t in range(GROUP):
            hail(8 * upper + t, plane)

    above = plane + core + 2 - 8 * lax.div(plane + 2, 8)
    below = lax.rem(plane + 6, 8) + core
    for other in (above, below):
        pl.semaphore_signal(barrier, inc=1, device_id={"blk": b, "sims": other}, device_id_type=MESH)

    upper = lax.div(y, 2)
    own_y = jnp.where(upper == 1, 2 + core, 1 - core)
    slot = 4 * lax.rem(y, 2) + x

    def prepare_side(r):
        for copy in reads(r):
            copy.wait()
        high, low = split(diag_ref[r])
        diag_high[r] = high
        diag_low[r] = low
        side_out[r, :COLS] = rhs_ref[r].T
        row = 16 * r + b
        masks = []
        for k in (1, 2):
            column = jnp.full((1, BS), col_ref[k, 0, r], jnp.int32)
            for d in (2, 3, 4):
                masks.append(jnp.where((column >= 0) & (column == row - d), 1.0, 0.0).astype(F32))
        masks.append(jnp.zeros((2, BS), F32))
        side_out[r, COLS:] = jnp.concatenate(masks, 0)

    def prepare(r, k):
        high, low = diag_high[r, pl.ds(mine, 128), :], diag_low[r, pl.ds(mine, 128), :]
        both = jnp.concatenate([high, low], 0)
        l_high, l_low = split(lower_ref[r, k])
        wide = dot(both, l_high)
        push_out[r, k] = wide[:128] + (wide[128:] + dot(high, l_low))

    def owner_of(r, there):
        return {"blk": 4 * jnp.where(upper == 1, 2 + there, 1 - there) + r, "sims": plane + 1}

    def twin_copy(r):
        return pltpu.make_async_remote_copy(
            side_out.at[r], side_twin.at[r], twin_sent.at[r], twin_got.at[r],
            device_id={"blk": b, "sims": plane}, device_id_type=MESH,
        )

    def side_copies(r):
        return [
            pltpu.make_async_remote_copy(
                (side_out, side_twin)[there].at[r], side_in.at[slot], side_sent.at[r, there], side_got.at[slot],
                device_id=owner_of(r, there), device_id_type=MESH,
            )
            for there in (0, 1)
        ]

    def send_side(r):
        landed(side_twin.at[r], twin_got.at[r])
        for copy in side_copies(r):
            copy.start()

    def push_copies(r, k):
        return [
            pltpu.make_async_remote_copy(
                push_out.at[r, k], push_in.at[slot, k, pl.ds(mine, 128)], push_sent.at[r, k, there], push_got.at[slot, k],
                device_id=owner_of(r, there), device_id_type=MESH,
            )
            for there in (0, 1)
        ]

    def quarter(t, k, n):
        where = push_in.at[t, k, pl.ds(mine + 64 * n, 64)]
        return pltpu.make_async_remote_copy(
            where, where, pass_sent.at[t, k, n], pass_got.at[t, k, n],
            device_id={"blk": b, "sims": (above, below)[n]}, device_id_type=MESH,
        )

    def keep(t, k, start):
        rows = pl.ds(start, 128)
        high, low = split(push_in[t, k, rows, :])
        push_high[t, k, rows, :] = high
        push_low[t, k, rows, :] = low

    def forward(step, carry):
        k, t = lax.div(step, GROUP), GROUP - 1 - lax.rem(step, GROUP)
        landed(push_in.at[t, k, pl.ds(mine, 128)], push_got.at[t, k])
        for n in range(2):
            quarter(t, k, n).start()
        keep(t, k, mine)
        return carry

    def receive_all(k):
        theirs = pl.multiple_of(128 - mine, 128)

        def one(step, carry):
            t = GROUP - 1 - step
            for n in range(2):
                landed(push_in.at[t, k, pl.ds(theirs + 64 * n, 64)], pass_got.at[t, k, n])
            keep(t, k, theirs)
            return carry

        lax.fori_loop(0, GROUP, one, 0)

    def forward_all(k):
        def one(step, carry):
            forward(k * GROUP + step, 0)
            return carry

        lax.fori_loop(0, GROUP, one, 0)

    def sent_push(k):
        def one(r, carry):
            for copy in push_copies(r, k):
                copy.wait_send()
            return carry

        lax.fori_loop(0, ROWS, one, 0)

    def push_all(k):
        def one(step, carry):
            r = 3 - step
            prepare(r, k)
            for copy in push_copies(r, k):
                copy.start()
            return carry

        lax.fori_loop(0, ROWS, one, 0)

    def prepare_sides(step, carry):
        prepare_side(3 - step)
        return carry

    columns.wait()
    lax.fori_loop(0, 1, prepare_sides, 0)

    @pl.when(core == 0)
    def _():
        prepare(3, 0)

    pl.semaphore_wait(barrier, NB + 1 + 2 * ROWS)

    @pl.when(core == 0)
    def _():
        for copy in push_copies(3, 0):
            copy.start()

    lax.fori_loop(1, ROWS, prepare_sides, 0)

    @pl.when(core == 0)
    def _():
        def first(step, carry):
            r = 2 - step
            prepare(r, 0)
            for copy in push_copies(r, 0):
                copy.start()
            return carry

        lax.fori_loop(0, 3, first, 0)
        push_all(1)
        push_all(2)
        send_side(3)
        for k in range(KMAX):
            sent_push(k)
        for r in (2, 1, 0):
            send_side(r)

    @pl.when(core == 1)
    def _():
        @pl.when((upper == 1) & (x == 3))
        def _():
            edge_out[...] = jnp.zeros_like(edge_out)
            for p in range(PIECES):
                for d in range(4):
                    pltpu.make_async_copy(edge_out.at[p, d], edge_in.at[p, d], edge_got.at[p, d]).start()

        for r in range(ROWS):
            twin_copy(r).start()
        forward_all(0)
        forward_all(1)
        receive_all(0)
        forward_all(2)
        receive_all(1)
        receive_all(2)

    for copy in small:
        copy.wait()

    def members(r):
        ids = dist_ref[r]
        return lax.broadcasted_iota(jnp.int32, (NDIST, BS), 0) == ids

    numer[...] = jnp.zeros_like(numer)

    def exchange(source, target, sent, got):
        def one(step, carry):
            other = lax.rem(b + step, NB)
            pltpu.make_async_remote_copy(
                source.at[pl.ds(SHARE * other, SHARE)], target.at[b], sent.at[other], got.at[b],
                device_id={"blk": other, "sims": s}, device_id_type=MESH,
            ).start()
            return carry

        lax.fori_loop(1, NB, one, 0, unroll=True)
        target[b] = source[pl.ds(pl.multiple_of(SHARE * b, SHARE), SHARE), :]

    def exchanged(source, target, sent, got):
        def one(step, carry):
            other = lax.rem(b + step, NB)
            landed(target.at[other], got.at[other])
            landed(source.at[pl.ds(SHARE * other, SHARE)], sent.at[other])
            return carry

        lax.fori_loop(1, NB, one, 0, unroll=True)

    def share_weights():
        weight = jnp.zeros((NDIST, BS), F32)
        for r in range(ROWS):
            weight = weight + jnp.where(members(r), turn_ref[r], 0.0)
        denom[...] = jnp.broadcast_to(jnp.sum(weight, 1, keepdims=True), (NDIST, COLS))
        exchange(denom, denom_in, denom_sent, denom_got)

    @pl.when((core == 0) | (x < 3))
    def _():
        share_weights()

    def finish(r):
        landed(zeta_in.at[r], zeta_got.at[r])
        high, low = split(zeta_in[r])
        both = jnp.concatenate([high, low], 0)
        wide = dot(both, diag_high[r])
        field = wide[:COLS] + (wide[COLS:] + dot(high, diag_low[r]))
        sol_ref[r] = field.T
        w_high, w_low = split(field * turn_ref[r])
        member = jnp.where(members(r), 1.0, 0.0).astype(BF16)
        contract = (((1,), (1,)), ((), ()))
        numer[...] += lax.dot_general(
            member, w_high, contract, preferred_element_type=F32
        ) + lax.dot_general(member, w_low, contract, preferred_element_type=F32)

    def finish_down(step, carry):
        finish(3 - step)
        return carry

    @pl.when(core == 0)
    def _():
        lax.fori_loop(0, ROWS, finish_down, 0)

    @pl.when(core == 1)
    def _():
        half = lax.div(y, 2)
        part = jnp.where(half == 1, lax.rem(y, 2), 1 - lax.rem(y, 2))
        is_last = (half == 0) & (x == 0)
        next_b = jnp.where(half == 1, 4 * (1 - part) + x, 4 * (2 + part) + x - 1)

        early = jnp.maximum(2 - x, 0)
        def receive_side(t, carry):
            landed(side_in.at[t], side_got.at[t])
            return carry

        lax.fori_loop(0, GROUP, receive_side, 0)

        def edge_copy(p, d):
            return pltpu.make_async_remote_copy(
                edge_out.at[p, d], edge_in.at[p, d], edge_sent.at[p, d], edge_got.at[p, d],
                device_id={"blk": next_b, "sims": s}, device_id_type=MESH,
            )

        def home(t):
            return 4 * (2 * half + lax.div(t, 4)) + lax.rem(t, 4)

        def is_home(t):
            return (part == 1) & (home(t) == b)

        def return_zeta(rows):
            def one(step, carry):
                t = GROUP - 1 - step
                src, dst = zeta.at[t, rows], zeta_in.at[x, rows]

                @pl.when(is_home(t))
                def _():
                    pltpu.make_async_copy(src, dst, zeta_got.at[x]).start()

                @pl.when(jnp.logical_not(is_home(t)))
                def _():
                    pltpu.make_async_remote_copy(
                        src, dst, zeta_sent.at[t], zeta_got.at[x],
                        device_id={"blk": home(t), "sims": plane + part}, device_id_type=MESH,
                    ).start()

                return carry

            lax.fori_loop(0, GROUP, one, 0)

        def piece(p, carry):
            here = pl.ds(pl.multiple_of(WIDTH * p, WIDTH), WIDTH)

            def far(t, both, high, pending):
                updates = []
                for k in (1, 2):
                    wide = dot(both, push_high[t, k])
                    updates.append(wide[:WIDTH] + (wide[WIDTH:] + dot(high, push_low[t, k])))
                for d in range(3):
                    first = side_in[t, COLS + d : COLS + d + 1, :] > 0.5
                    second = side_in[t, COLS + 3 + d : COLS + 4 + d, :] > 0.5
                    update = jnp.where(first, updates[0], jnp.where(second, updates[1], 0.0))
                    row = t - 2 - d
                    pending[row] = pending[row] + update if row in pending else update

            pending = {}
            for t in reversed(range(GROUP)):
                d = GROUP - 1 - t
                if d < 4:
                    landed(edge_in.at[p, d], edge_got.at[p, d])
                    edge = edge_in[p, d]
                    pending[t] = pending[t] + edge if t in pending else edge
                z = side_in[t, here, :] - pending[t]
                zeta[t, here, :] = z
                high, low = split(z)
                both = jnp.concatenate([high, low], 0)
                wide = dot(both, push_high[t, 0])
                low_part = dot(high, push_low[t, 0])
                update = wide[:WIDTH] + (wide[WIDTH:] + low_part)
                far(t, both, high, pending)
                pending[t - 1] = pending[t - 1] + update if t - 1 in pending else update
            edge_out[p, 0] = pending[-1]

            @pl.when(jnp.logical_not(is_last))
            def _():
                edge_copy(p, 0).start()

            for d in range(1, 4):
                edge_out[p, d] = pending[-1 - d]

            @pl.when(jnp.logical_not(is_last))
            def _():
                for d in range(1, 4):
                    edge_copy(p, d).start()

            @pl.when(is_last)
            def _():
                return_zeta(here)

            return carry

        lax.fori_loop(0, early, finish_down, 0)
        lax.fori_loop(0, PIECES, piece, 0)

        @pl.when(jnp.logical_not(is_last))
        def _():
            return_zeta(pl.ds(0, COLS))


        @pl.when(x == 3)
        def _():
            share_weights()

        lax.fori_loop(early, ROWS, finish_down, 0)

        @pl.when(jnp.logical_not(is_last))
        def _():
            for p in range(PIECES):
                for d in range(4):
                    edge_copy(p, d).wait_send()

        def sent_one(t, c):
            @pl.when(jnp.logical_not(is_home(t)))
            def _():
                landed(zeta.at[t], zeta_sent.at[t])

            return c

        lax.fori_loop(0, GROUP, sent_one, 0)

        def passed(t, c):
            for k in range(KMAX):
                for n in range(2):
                    quarter(t, k, n).wait_send()
            return c

        lax.fori_loop(0, GROUP, passed, 0)

    exchange(numer, numer_in, numer_sent, numer_got)

    @pl.when(core == 0)
    def _():
        def sent_side(r, carry):
            for copy in side_copies(r):
                copy.wait_send()
            return carry

        lax.fori_loop(0, ROWS, sent_side, 0)

    @pl.when(core == 1)
    def _():
        def sent_twin(r, carry):
            twin_copy(r).wait_send()
            return carry

        lax.fori_loop(0, ROWS, sent_twin, 0)

    exchanged(denom, denom_in, denom_sent, denom_got)
    exchanged(numer, numer_in, numer_sent, numer_got)
    mean_ref[...] = jnp.sum(numer_in[...], 0) / jnp.sum(denom_in[...], 0)


def body(rhs, lower_blocks, col_index, diag_inverse, turnout, district_of):
    vmem = pl.BlockSpec(memory_space=pltpu.VMEM)
    hbm = pl.BlockSpec(memory_space=pltpu.HBM)
    dma = pltpu.SemaphoreType.DMA
    field, mean = pl.pallas_call(
        kernel,
        out_shape=(
            jax.ShapeDtypeStruct((ROWS, BS, COLS), F32),
            jax.ShapeDtypeStruct((SHARE, COLS), F32),
        ),
        in_specs=[hbm, hbm, hbm, hbm, hbm, hbm],
        out_specs=(vmem, vmem),
        scratch_shapes=[
            pltpu.VMEM((ROWS, BS, COLS), F32),
            pltpu.VMEM((ROWS, KMAX, BS, BS), F32),
            pltpu.VMEM((ROWS, BS, BS), F32),
            pltpu.VMEM((ROWS, 1, BS), F32),
            pltpu.VMEM((ROWS, 1, BS), jnp.int32),
            pltpu.SMEM((KMAX, 1, ROWS), jnp.int32),
            pltpu.VMEM((ROWS, BS, BS), BF16),
            pltpu.VMEM((ROWS, BS, BS), BF16),
            pltpu.VMEM((ROWS, KMAX, BS // 2, BS), F32),
            pltpu.VMEM((ROWS, COLS + 8, BS), F32),
            pltpu.VMEM((ROWS, COLS + 8, BS), F32),
            pltpu.VMEM((GROUP, KMAX, BS, BS), F32),
            pltpu.VMEM((GROUP, COLS + 8, BS), F32),
            pltpu.VMEM((GROUP, KMAX, BS, BS), BF16),
            pltpu.VMEM((GROUP, KMAX, BS, BS), BF16),
            pltpu.VMEM((GROUP, COLS, BS), F32),
            pltpu.VMEM((ROWS, COLS, BS), F32),
            pltpu.VMEM((PIECES, 4, WIDTH, BS), F32),
            pltpu.VMEM((PIECES, 4, WIDTH, BS), F32),
            pltpu.VMEM((NDIST, COLS), F32),
            pltpu.VMEM((NB, SHARE, COLS), F32),
            pltpu.VMEM((NDIST, COLS), F32),
            pltpu.VMEM((NB, SHARE, COLS), F32),
            dma((ROWS, 3)), dma((3,)), dma((ROWS, KMAX, 2)), dma((GROUP, KMAX)), dma((GROUP, KMAX, 2)), dma((GROUP, KMAX, 2)),
            dma((ROWS,)), dma((ROWS,)), dma((ROWS, 2)), dma((GROUP,)), dma((PIECES, 4)), dma((PIECES, 4)),
            dma((GROUP,)), dma((ROWS,)),
            dma((NB,)), dma((NB,)), dma((NB,)), dma((NB,)),
        ],
        name="back_substitution",
        compiler_params=pltpu.CompilerParams(
            collective_id=0, has_side_effects=True, vmem_limit_bytes=48 * 1024 * 1024
        ),
    )(
        in_hbm(rhs), in_hbm(lower_blocks), in_hbm(jnp.transpose(col_index, (2, 1, 0))), in_hbm(diag_inverse),
        in_hbm(turnout), in_hbm(district_of),
    )
    return field[:, None], mean


def solution(mesh):
    placed = (
        P(None, "blk", None, "sims"),
        P(None, "blk", None, None, None),
        P(None, "blk", None),
        P(None, "blk", None, None),
        P(None, "blk", None),
        P(None, "blk", None),
    )
    return jax.shard_map(
        body,
        mesh=mesh,
        in_specs=placed,
        out_specs=(P(None, "blk", None, "sims"), P("blk", "sims")),
        check_vma=False,
    )
```

```python
import jax
import jax.numpy as jnp
from jax import lax
from jax.experimental import pallas as pl
from jax.experimental.pallas import tpu as pltpu
from jax.sharding import PartitionSpec as P

MESH = pl.DeviceIdType.MESH
F32 = jnp.float32
BF16 = jnp.bfloat16

BS = 256
ROWS = 4
KMAX = 3
COLS = 128
NB = 16
NDIST = 256
SHARE = NDIST // NB
GROUP = 8
PIECES = 4
WIDTH = COLS // PIECES


def split(value):
    high = value.astype(BF16)
    return high, (value - high.astype(F32)).astype(BF16)


def dot(a, b):
    return jnp.dot(a, b, preferred_element_type=F32)


def landed(ref, sem):
    pltpu.make_async_copy(ref, ref, sem).wait()


def in_hbm(array):
    return pltpu.with_memory_space_constraint(array, pltpu.HBM)


def kernel(
    rhs_hbm, lower_hbm, col_hbm, diag_hbm, turn_hbm, dist_hbm,
    sol_ref, mean_ref,
    rhs_ref, lower_ref, diag_ref, turn_ref, dist_ref, col_ref,
    diag_high, diag_low, push_out, side_out, side_twin, push_in, side_in, push_high, push_low,
    zeta, zeta_in, edge_in, edge_out, numer, numer_in, denom, denom_in,
    read_got, small_got, push_sent, push_got, pass_sent, pass_got, twin_sent, twin_got, side_sent, side_got, edge_sent, edge_got,
    zeta_sent, zeta_got, numer_sent, numer_got, denom_sent, denom_got,
):
    b = lax.axis_index("blk")
    s = lax.axis_index("sims")
    y, x = lax.div(b, 4), lax.rem(b, 4)
    core = lax.rem(s, 2)
    plane = s - core
    z_here = lax.div(s, 2)
    mine = pl.multiple_of(128 * lax.rem(z_here, 2), 128)

    def reads(r):
        return (
            pltpu.make_async_copy(diag_hbm.at[r, 0], diag_ref.at[r], read_got.at[r, 0]),
            pltpu.make_async_copy(lower_hbm.at[r, 0], lower_ref.at[r], read_got.at[r, 1]),
            pltpu.make_async_copy(rhs_hbm.at[r, 0], rhs_ref.at[r], read_got.at[r, 2]),
        )

    def start_reads(step, carry):
        for copy in reads(3 - step):
            copy.start()
        return carry

    columns = pltpu.make_async_copy(col_hbm, col_ref, small_got.at[2])
    columns.start()
    lax.fori_loop(0, 1, start_reads, 0)
    small = (
        pltpu.make_async_copy(turn_hbm, turn_ref, small_got.at[0]),
        pltpu.make_async_copy(dist_hbm, dist_ref, small_got.at[1]),
    )

    barrier = pltpu.get_barrier_semaphore()

    def hail(other_blk, other_sims):
        pl.semaphore_signal(barrier, inc=1, device_id={"blk": other_blk, "sims": other_sims}, device_id_type=MESH)

    upper = lax.div(y, 2)
    lane = jnp.where(upper == 1, lax.rem(y, 2), 1 - lax.rem(y, 2))

    def greet(step, carry):
        hail(lax.rem(b + step, NB), s)
        return carry

    lax.fori_loop(1, NB, greet, 0)

    @pl.when(core == 0)
    def _():
        for r in range(ROWS):
            for there in (0, 1):
                hail(4 * jnp.where(upper == 1, 2 + there, 1 - there) + r, plane + 1)

    @pl.when(core == 1)
    def _():
        for t in range(GROUP):
            hail(8 * upper + t, plane)

    above = plane + core + 2 - 8 * lax.div(plane + 2, 8)
    below = lax.rem(plane + 6, 8) + core
    for other in (above, below):
        pl.semaphore_signal(barrier, inc=1, device_id={"blk": b, "sims": other}, device_id_type=MESH)

    upper = lax.div(y, 2)
    own_y = jnp.where(upper == 1, 2 + core, 1 - core)
    slot = 4 * lax.rem(y, 2) + x

    lax.fori_loop(1, ROWS, start_reads, 0)
    for copy in small:
        copy.start()

    def prepare_side(r):
        for copy in reads(r):
            copy.wait()
        high, low = split(diag_ref[r])
        diag_high[r] = high
        diag_low[r] = low
        side_out[r, :COLS] = rhs_ref[r].T
        row = 16 * r + b
        masks = []
        for k in (1, 2):
            column = jnp.full((1, BS), col_ref[k, 0, r], jnp.int32)
            for d in (2, 3, 4):
                masks.append(jnp.where((column >= 0) & (column == row - d), 1.0, 0.0).astype(F32))
        masks.append(jnp.zeros((2, BS), F32))
        side_out[r, COLS:] = jnp.concatenate(masks, 0)

    def prepare(r, k):
        high, low = diag_high[r, pl.ds(mine, 128), :], diag_low[r, pl.ds(mine, 128), :]
        both = jnp.concatenate([high, low], 0)
        l_high, l_low = split(lower_ref[r, k])
        wide = dot(both, l_high)
        push_out[r, k] = wide[:128] + (wide[128:] + dot(high, l_low))

    def owner_of(r, there):
        return {"blk": 4 * jnp.where(upper == 1, 2 + there, 1 - there) + r, "sims": plane + 1}

    def twin_copy(r):
        return pltpu.make_async_remote_copy(
            side_out.at[r], side_twin.at[r], twin_sent.at[r], twin_got.at[r],
            device_id={"blk": b, "sims": plane}, device_id_type=MESH,
        )

    def side_copies(r):
        return [
            pltpu.make_async_remote_copy(
                (side_out, side_twin)[there].at[r], side_in.at[slot], side_sent.at[r, there], side_got.at[slot],
                device_id=owner_of(r, there), device_id_type=MESH,
            )
            for there in (0, 1)
        ]

    def send_side(r):
        landed(side_twin.at[r], twin_got.at[r])
        for copy in side_copies(r):
            copy.start()

    def push_copies(r, k):
        return [
            pltpu.make_async_remote_copy(
                push_out.at[r, k], push_in.at[slot, k, pl.ds(mine, 128)], push_sent.at[r, k, there], push_got.at[slot, k],
                device_id=owner_of(r, there), device_id_type=MESH,
            )
            for there in (0, 1)
        ]

    def quarter(t, k, n):
        where = push_in.at[t, k, pl.ds(mine + 64 * n, 64)]
        return pltpu.make_async_remote_copy(
            where, where, pass_sent.at[t, k, n], pass_got.at[t, k, n],
            device_id={"blk": b, "sims": (above, below)[n]}, device_id_type=MESH,
        )

    def keep(t, k, start):
        rows = pl.ds(start, 128)
        high, low = split(push_in[t, k, rows, :])
        push_high[t, k, rows, :] = high
        push_low[t, k, rows, :] = low

    def forward(step, carry):
        k, t = lax.div(step, GROUP), GROUP - 1 - lax.rem(step, GROUP)
        landed(push_in.at[t, k, pl.ds(mine, 128)], push_got.at[t, k])
        for n in range(2):
            quarter(t, k, n).start()
        keep(t, k, mine)
        return carry

    def receive_all(k):
        theirs = pl.multiple_of(128 - mine, 128)

        def one(step, carry):
            t = GROUP - 1 - step
            for n in range(2):
                landed(push_in.at[t, k, pl.ds(theirs + 64 * n, 64)], pass_got.at[t, k, n])
            keep(t, k, theirs)
            return carry

        lax.fori_loop(0, GROUP, one, 0)

    def forward_all(k):
        def one(step, carry):
            forward(k * GROUP + step, 0)
            return carry

        lax.fori_loop(0, GROUP, one, 0)

    def sent_push(k):
        def one(r, carry):
            for copy in push_copies(r, k):
                copy.wait_send()
            return carry

        lax.fori_loop(0, ROWS, one, 0)

    def push_all(k):
        def one(step, carry):
            r = 3 - step
            prepare(r, k)
            for copy in push_copies(r, k):
                copy.start()
            return carry

        lax.fori_loop(0, ROWS, one, 0)

    def prepare_sides(step, carry):
        prepare_side(3 - step)
        return carry

    columns.wait()
    lax.fori_loop(0, 1, prepare_sides, 0)

    @pl.when(core == 0)
    def _():
        prepare(3, 0)

    pl.semaphore_wait(barrier, NB + 1 + 2 * ROWS)

    @pl.when(core == 0)
    def _():
        for copy in push_copies(3, 0):
            copy.start()

    lax.fori_loop(1, ROWS, prepare_sides, 0)

    @pl.when(core == 0)
    def _():
        def first(step, carry):
            r = 2 - step
            prepare(r, 0)
            for copy in push_copies(r, 0):
                copy.start()
            return carry

        lax.fori_loop(0, 3, first, 0)
        push_all(1)
        push_all(2)
        send_side(3)
        for k in range(KMAX):
            sent_push(k)
        for r in (2, 1, 0):
            send_side(r)

    @pl.when(core == 1)
    def _():
        @pl.when((upper == 1) & (x == 3))
        def _():
            edge_out[...] = jnp.zeros_like(edge_out)
            for p in range(PIECES):
                for d in range(4):
                    pltpu.make_async_copy(edge_out.at[p, d], edge_in.at[p, d], edge_got.at[p, d]).start()

        for r in range(ROWS):
            twin_copy(r).start()
        forward_all(0)
        forward_all(1)
        receive_all(0)
        forward_all(2)
        receive_all(1)
        receive_all(2)

    for copy in small:
        copy.wait()

    def members(r):
        ids = dist_ref[r]
        return lax.broadcasted_iota(jnp.int32, (NDIST, BS), 0) == ids

    numer[...] = jnp.zeros_like(numer)

    def exchange(source, target, sent, got):
        def one(step, carry):
            other = lax.rem(b + step, NB)
            pltpu.make_async_remote_copy(
                source.at[pl.ds(SHARE * other, SHARE)], target.at[b], sent.at[other], got.at[b],
                device_id={"blk": other, "sims": s}, device_id_type=MESH,
            ).start()
            return carry

        lax.fori_loop(1, NB, one, 0, unroll=True)
        target[b] = source[pl.ds(pl.multiple_of(SHARE * b, SHARE), SHARE), :]

    def exchanged(source, target, sent, got):
        def one(step, carry):
            other = lax.rem(b + step, NB)
            landed(target.at[other], got.at[other])
            landed(source.at[pl.ds(SHARE * other, SHARE)], sent.at[other])
            return carry

        lax.fori_loop(1, NB, one, 0, unroll=True)

    def share_weights():
        weight = jnp.zeros((NDIST, BS), F32)
        for r in range(ROWS):
            weight = weight + jnp.where(members(r), turn_ref[r], 0.0)
        denom[...] = jnp.broadcast_to(jnp.sum(weight, 1, keepdims=True), (NDIST, COLS))
        exchange(denom, denom_in, denom_sent, denom_got)

    @pl.when((core == 0) | (x < 3))
    def _():
        share_weights()

    def finish(r):
        landed(zeta_in.at[r], zeta_got.at[r])
        high, low = split(zeta_in[r])
        both = jnp.concatenate([high, low], 0)
        wide = dot(both, diag_high[r])
        field = wide[:COLS] + (wide[COLS:] + dot(high, diag_low[r]))
        sol_ref[r] = field.T
        w_high, w_low = split(field * turn_ref[r])
        member = jnp.where(members(r), 1.0, 0.0).astype(BF16)
        contract = (((1,), (1,)), ((), ()))
        numer[...] += lax.dot_general(
            member, w_high, contract, preferred_element_type=F32
        ) + lax.dot_general(member, w_low, contract, preferred_element_type=F32)

    def finish_down(step, carry):
        finish(3 - step)
        return carry

    @pl.when(core == 0)
    def _():
        lax.fori_loop(0, ROWS, finish_down, 0)

    @pl.when(core == 1)
    def _():
        half = lax.div(y, 2)
        part = jnp.where(half == 1, lax.rem(y, 2), 1 - lax.rem(y, 2))
        is_last = (half == 0) & (x == 0)
        next_b = jnp.where(half == 1, 4 * (1 - part) + x, 4 * (2 + part) + x - 1)

        early = jnp.maximum(2 - x, 0)
        def receive_side(t, carry):
            landed(side_in.at[t], side_got.at[t])
            return carry

        lax.fori_loop(0, GROUP, receive_side, 0)

        def edge_copy(p, d):
            return pltpu.make_async_remote_copy(
                edge_out.at[p, d], edge_in.at[p, d], edge_sent.at[p, d], edge_got.at[p, d],
                device_id={"blk": next_b, "sims": s}, device_id_type=MESH,
            )

        def home(t):
            return 4 * (2 * half + lax.div(t, 4)) + lax.rem(t, 4)

        def is_home(t):
            return (part == 1) & (home(t) == b)

        def return_zeta(rows):
            def one(step, carry):
                t = GROUP - 1 - step
                src, dst = zeta.at[t, rows], zeta_in.at[x, rows]

                @pl.when(is_home(t))
                def _():
                    pltpu.make_async_copy(src, dst, zeta_got.at[x]).start()

                @pl.when(jnp.logical_not(is_home(t)))
                def _():
                    pltpu.make_async_remote_copy(
                        src, dst, zeta_sent.at[t], zeta_got.at[x],
                        device_id={"blk": home(t), "sims": plane + part}, device_id_type=MESH,
                    ).start()

                return carry

            lax.fori_loop(0, GROUP, one, 0)

        def piece(p, carry):
            here = pl.ds(pl.multiple_of(WIDTH * p, WIDTH), WIDTH)

            def far(t, both, high, pending):
                updates = []
                for k in (1, 2):
                    wide = dot(both, push_high[t, k])
                    updates.append(wide[:WIDTH] + (wide[WIDTH:] + dot(high, push_low[t, k])))
                for d in range(3):
                    first = side_in[t, COLS + d : COLS + d + 1, :] > 0.5
                    second = side_in[t, COLS + 3 + d : COLS + 4 + d, :] > 0.5
                    update = jnp.where(first, updates[0], jnp.where(second, updates[1], 0.0))
                    row = t - 2 - d
                    pending[row] = pending[row] + update if row in pending else update

            pending = {}
            for t in reversed(range(GROUP)):
                d = GROUP - 1 - t
                if d < 4:
                    landed(edge_in.at[p, d], edge_got.at[p, d])
                    edge = edge_in[p, d]
                    pending[t] = pending[t] + edge if t in pending else edge
                z = side_in[t, here, :] - pending[t]
                zeta[t, here, :] = z
                high, low = split(z)
                both = jnp.concatenate([high, low], 0)
                wide = dot(both, push_high[t, 0])
                low_part = dot(high, push_low[t, 0])
                update = wide[:WIDTH] + (wide[WIDTH:] + low_part)
                far(t, both, high, pending)
                pending[t - 1] = pending[t - 1] + update if t - 1 in pending else update
            edge_out[p, 0] = pending[-1]

            @pl.when(jnp.logical_not(is_last))
            def _():
                edge_copy(p, 0).start()

            for d in range(1, 4):
                edge_out[p, d] = pending[-1 - d]

            @pl.when(jnp.logical_not(is_last))
            def _():
                for d in range(1, 4):
                    edge_copy(p, d).start()

            @pl.when(is_last)
            def _():
                return_zeta(here)

            return carry

        lax.fori_loop(0, early, finish_down, 0)
        lax.fori_loop(0, PIECES, piece, 0)

        @pl.when(jnp.logical_not(is_last))
        def _():
            return_zeta(pl.ds(0, COLS))


        @pl.when(x == 3)
        def _():
            share_weights()

        lax.fori_loop(early, ROWS, finish_down, 0)

        @pl.when(jnp.logical_not(is_last))
        def _():
            for p in range(PIECES):
                for d in range(4):
                    edge_copy(p, d).wait_send()

        def sent_one(t, c):
            @pl.when(jnp.logical_not(is_home(t)))
            def _():
                landed(zeta.at[t], zeta_sent.at[t])

            return c

        lax.fori_loop(0, GROUP, sent_one, 0)

        def passed(t, c):
            for k in range(KMAX):
                for n in range(2):
                    quarter(t, k, n).wait_send()
            return c

        lax.fori_loop(0, GROUP, passed, 0)

    exchange(numer, numer_in, numer_sent, numer_got)

    @pl.when(core == 0)
    def _():
        def sent_side(r, carry):
            for copy in side_copies(r):
                copy.wait_send()
            return carry

        lax.fori_loop(0, ROWS, sent_side, 0)

    @pl.when(core == 1)
    def _():
        def sent_twin(r, carry):
            twin_copy(r).wait_send()
            return carry

        lax.fori_loop(0, ROWS, sent_twin, 0)

    exchanged(denom, denom_in, denom_sent, denom_got)
    exchanged(numer, numer_in, numer_sent, numer_got)
    mean_ref[...] = jnp.sum(numer_in[...], 0) / jnp.sum(denom_in[...], 0)


def body(rhs, lower_blocks, col_index, diag_inverse, turnout, district_of):
    vmem = pl.BlockSpec(memory_space=pltpu.VMEM)
    hbm = pl.BlockSpec(memory_space=pltpu.HBM)
    dma = pltpu.SemaphoreType.DMA
    field, mean = pl.pallas_call(
        kernel,
        out_shape=(
            jax.ShapeDtypeStruct((ROWS, BS, COLS), F32),
            jax.ShapeDtypeStruct((SHARE, COLS), F32),
        ),
        in_specs=[hbm, hbm, hbm, hbm, hbm, hbm],
        out_specs=(vmem, vmem),
        scratch_shapes=[
            pltpu.VMEM((ROWS, BS, COLS), F32),
            pltpu.VMEM((ROWS, KMAX, BS, BS), F32),
            pltpu.VMEM((ROWS, BS, BS), F32),
            pltpu.VMEM((ROWS, 1, BS), F32),
            pltpu.VMEM((ROWS, 1, BS), jnp.int32),
            pltpu.SMEM((KMAX, 1, ROWS), jnp.int32),
            pltpu.VMEM((ROWS, BS, BS), BF16),
            pltpu.VMEM((ROWS, BS, BS), BF16),
            pltpu.VMEM((ROWS, KMAX, BS // 2, BS), F32),
            pltpu.VMEM((ROWS, COLS + 8, BS), F32),
            pltpu.VMEM((ROWS, COLS + 8, BS), F32),
            pltpu.VMEM((GROUP, KMAX, BS, BS), F32),
            pltpu.VMEM((GROUP, COLS + 8, BS), F32),
            pltpu.VMEM((GROUP, KMAX, BS, BS), BF16),
            pltpu.VMEM((GROUP, KMAX, BS, BS), BF16),
            pltpu.VMEM((GROUP, COLS, BS), F32),
            pltpu.VMEM((ROWS, COLS, BS), F32),
            pltpu.VMEM((PIECES, 4, WIDTH, BS), F32),
            pltpu.VMEM((PIECES, 4, WIDTH, BS), F32),
            pltpu.VMEM((NDIST, COLS), F32),
            pltpu.VMEM((NB, SHARE, COLS), F32),
            pltpu.VMEM((NDIST, COLS), F32),
            pltpu.VMEM((NB, SHARE, COLS), F32),
            dma((ROWS, 3)), dma((3,)), dma((ROWS, KMAX, 2)), dma((GROUP, KMAX)), dma((GROUP, KMAX, 2)), dma((GROUP, KMAX, 2)),
            dma((ROWS,)), dma((ROWS,)), dma((ROWS, 2)), dma((GROUP,)), dma((PIECES, 4)), dma((PIECES, 4)),
            dma((GROUP,)), dma((ROWS,)),
            dma((NB,)), dma((NB,)), dma((NB,)), dma((NB,)),
        ],
        name="back_substitution",
        compiler_params=pltpu.CompilerParams(
            collective_id=0, has_side_effects=True, vmem_limit_bytes=48 * 1024 * 1024
        ),
    )(
        in_hbm(rhs), in_hbm(lower_blocks), in_hbm(jnp.transpose(col_index, (2, 1, 0))), in_hbm(diag_inverse),
        in_hbm(turnout), in_hbm(district_of),
    )
    return field[:, None], mean


def solution(mesh):
    placed = (
        P(None, "blk", None, "sims"),
        P(None, "blk", None, None, None),
        P(None, "blk", None),
        P(None, "blk", None, None),
        P(None, "blk", None),
        P(None, "blk", None),
    )
    return jax.shard_map(
        body,
        mesh=mesh,
        in_specs=placed,
        out_specs=(P(None, "blk", None, "sims"), P("blk", "sims")),
        check_vma=False,
    )
```
